32 devices in a mesh: row: 4 (over z), col: 8 (over y, x, core).
Axes of the slice: x: 2, y: 2, z: 4, core: 2. Of those that a mesh axis runs over, the one named last changes fastest.
Arguments:
- obj_re: float32 [2048, 4096], P('row', 'col'), may hold values from -4 to 4
- obj_im: float32 [2048, 4096], P('row', 'col'), may hold values from -4 to 4
- probe_re: float32 [512, 512], replicated, may hold values from -6 to 6
- probe_im: float32 [512, 512], replicated, may hold values from -6 to 6
- amplitude: bfloat16 [4, 32, 512, 512], P('row', 'col'), may hold values from 0.099609375 to 3
- offset_y: int32 [4, 32], P('row', 'col'), may hold values from 0 to 511
- offset_x: int32 [4, 32], P('row', 'col'), may hold values from 0 to 511
- counts: int32 [4, 8], P('row', 'col'), may hold values from 1 to 4, as said below
Outputs:
- new_re: float32 [2048, 4096], P('row', 'col')
- new_im: float32 [2048, 4096], P('row', 'col')
The draws below stay inside these ranges and needn't reach their ends.
Inputs may be any that keep to these rules, and one draw needn't show every extreme that they name: The live slots of a device are its first counts[r, c] slots; some device has 4 live slots. `offset_y`: A window starts inside the tile of the device that holds its slot.
All inputs are finite; a program needn't handle non-finite values.
Results may differ from the reference program's by a relative error of at most 0.0024.
The reference program's roundings to bfloat16 on the way count: a program that leaves them out, or rounds other values in their place, can miss the bound.
Values may be sent and summed in bfloat16 or wider, within the bound.
No kernel may reach another device: no remote copies, remote signals or barrier semaphores. Data moves between devices by JAX's collectives and lax.ppermute only.
A program may use at most 128 MiB of HBM per device.

```python
import math
import jax
import jax.numpy as jnp
from jax import lax

P_SIZE = 512
SLOT_DEV = 4
NY = 2048
NX = 4096
SLOT_COLS = 32
N_ROW = 4
N_COL = 8


def draw_counts(key, part):
    first_key, second_key = jax.random.split(jax.random.fold_in(key, 11))
    level = jax.random.randint(first_key, (N_ROW, N_COL), 0, 8)
    live_count = 1 + SLOT_DEV * level * level // 64
    chosen = jax.random.randint(second_key, (), 0, N_ROW * N_COL)
    flat_counts = live_count.reshape(-1)
    flat_counts = jnp.where(jnp.arange(N_ROW * N_COL) == chosen, SLOT_DEV, flat_counts)
    return flat_counts.reshape(N_ROW, N_COL).astype(jnp.int32)


def place_ends(values, rng, least, high):
    longest = values.shape.index(max(values.shape))
    spots = []
    for shift in (0, 1):
        where = [jax.random.randint(jax.random.fold_in(rng, axis), (), 0, length) for axis, length in enumerate(values.shape)]
        where[longest] = (where[longest] + shift) % values.shape[longest]
        spots.append(tuple(where))
    return values.at[spots[0]].set(least).at[spots[1]].set(high)


def block_scale(rng, dims, pieces, smallest, high):
    loudness = 1.0
    for axis_at, shards_of in pieces:
        draws = jax.random.uniform(jax.random.fold_in(jax.random.fold_in(rng, 6), axis_at), (shards_of,), jnp.float32, smallest / len(pieces), high / len(pieces))
        loudness = loudness * jnp.repeat(jnp.exp(draws), dims[axis_at] // shards_of).reshape((-1,) + (1,) * (len(dims) - 1 - axis_at))
    return loudness


def scatter_about(own_key, shape, deviation, bound, pieces=(), kind=jnp.bfloat16):
    values = jax.random.normal(own_key, shape, jnp.float32) * deviation
    if len(pieces) > 0:
        values = block_scale(own_key, shape, pieces, -0.22, 0.18) * values
    return jnp.clip(values, min=-bound, max=bound).astype(kind)


def setup_inputs(seed: int = 0) -> dict:
    splits = jax.random.split(jax.random.key(seed), 9)
    obj_re = scatter_about(splits[0], (NY, NX), 0.5, 4.0, ((0, 4), (1, 8)), jnp.float32)
    obj_im = scatter_about(splits[1], (NY, NX), 0.5, 4.0, ((0, 4), (1, 8)), jnp.float32)
    probe_re = scatter_about(splits[2], (P_SIZE, P_SIZE), 1.0, 6.0, (), jnp.float32)
    probe_im = scatter_about(splits[3], (P_SIZE, P_SIZE), 1.0, 6.0, (), jnp.float32)
    amplitude = jnp.clip(jnp.exp(math.log(3.0) - 3.4051113 * jax.random.uniform(splits[4], (N_ROW, SLOT_COLS, P_SIZE, P_SIZE), jnp.float32) ** block_scale(splits[4], (N_ROW, SLOT_COLS, P_SIZE, P_SIZE), ((0, 4), (1, 8)), -0.2, 0.2)), 0.099609375, 3.0).astype(jnp.bfloat16)
    offset_y = place_ends(jax.random.randint(splits[5], (N_ROW, SLOT_COLS), 0, P_SIZE), jax.random.fold_in(splits[5], 1), 0, P_SIZE - 1).astype(jnp.int32)
    offset_x = place_ends(jax.random.randint(splits[6], (N_ROW, SLOT_COLS), 0, P_SIZE), jax.random.fold_in(splits[6], 1), 0, P_SIZE - 1).astype(jnp.int32)
    counts = draw_counts(jax.random.fold_in(splits[8], 71), 0)
    return dict(obj_re=obj_re, obj_im=obj_im, probe_re=probe_re, probe_im=probe_im, amplitude=amplitude, offset_y=offset_y, offset_x=offset_x, counts=counts)


modulus_floor = 0.5
shrink_level = 0.2
step_size = 0.5
epsilon = 1e-05

def dft_tables(pattern_side):
    ordinal = jnp.arange(pattern_side, dtype=jnp.int32)
    phase_index = ordinal[:, None] * ordinal[None, :] % pattern_side
    angles = phase_index.astype(jnp.float32) * (2.0 * math.pi / pattern_side)
    norming = 1.0 / math.sqrt(pattern_side)
    return ((jnp.cos(angles) * norming).astype(jnp.bfloat16), (-jnp.sin(angles) * norming).astype(jnp.bfloat16))

def matmul(left_op, right_op):
    return jnp.dot(left_op, right_op, preferred_element_type=jnp.float32)

def spectrum_rows(patch_tile, probe_re, probe_im, cos_table, sin_table):
    object_re = patch_tile[0].astype(jnp.float32)
    object_im = patch_tile[1].astype(jnp.float32)
    exit_re = (probe_re * object_re - probe_im * object_im).astype(jnp.bfloat16)
    exit_im = (probe_re * object_im + probe_im * object_re).astype(jnp.bfloat16)
    half_re = matmul(cos_table, exit_re) - matmul(sin_table, exit_im)
    half_im = matmul(cos_table, exit_im) + matmul(sin_table, exit_re)
    return jnp.stack([half_re, half_im]).astype(jnp.bfloat16)

def correct_rows(half_spec, measured, cos_table, sin_table):
    spec_re = matmul(half_spec[0], cos_table) - matmul(half_spec[1], sin_table)
    spec_im = matmul(half_spec[0], sin_table) + matmul(half_spec[1], cos_table)
    modulus = jnp.sqrt(spec_re * spec_re + spec_im * spec_im)
    factor = measured.astype(jnp.float32) / jnp.maximum(modulus, modulus_floor) - 1.0
    delta_re = (spec_re * factor).astype(jnp.bfloat16)
    delta_im = (spec_im * factor).astype(jnp.bfloat16)
    back_re = matmul(delta_re, cos_table) + matmul(delta_im, sin_table)
    back_im = matmul(delta_im, cos_table) - matmul(delta_re, sin_table)
    return jnp.stack([back_re, back_im]).astype(jnp.bfloat16)

def object_term(partial_back, probe_re, probe_im, cos_table, sin_table):
    wave_re = matmul(cos_table, partial_back[0]) + matmul(sin_table, partial_back[1])
    wave_im = matmul(cos_table, partial_back[1]) - matmul(sin_table, partial_back[0])
    return jnp.stack([probe_re * wave_re + probe_im * wave_im, probe_re * wave_im - probe_im * wave_re])

def shrink(entries):
    return entries - jnp.clip(entries, -shrink_level, shrink_level)

def haar_clean(field):
    top_left = field[:, 0::2, 0::2]
    top_right = field[:, 0::2, 1::2]
    low_left = field[:, 1::2, 0::2]
    low_right = field[:, 1::2, 1::2]
    coarse = 0.5 * (top_left + top_right + low_left + low_right)
    across = shrink(0.5 * (top_left - top_right + low_left - low_right))
    downward = shrink(0.5 * (top_left + top_right - low_left - low_right))
    diagonal = shrink(0.5 * (top_left - top_right - low_left + low_right))
    new_top_left = 0.5 * (coarse + across + downward + diagonal)
    new_top_right = 0.5 * (coarse - across + downward - diagonal)
    new_low_left = 0.5 * (coarse + across - downward - diagonal)
    new_low_right = 0.5 * (coarse - across - downward + diagonal)
    planes, height, breadth = top_left.shape
    top_rows = jnp.stack([new_top_left, new_top_right], axis=-1).reshape(planes, height, 2 * breadth)
    bottom_rows = jnp.stack([new_low_left, new_low_right], axis=-1).reshape(planes, height, 2 * breadth)
    return jnp.stack([top_rows, bottom_rows], axis=2).reshape(planes, 2 * height, 2 * breadth)

def reference(obj_re, obj_im, probe_re, probe_im, amplitude, offset_y, offset_x, counts):
    cos_table, sin_table = dft_tables(P_SIZE)
    probe_power = jnp.mean(probe_re * probe_re + probe_im * probe_im) + epsilon
    object_bf = jnp.stack([obj_re, obj_im]).astype(jnp.bfloat16)
    wrapped = jnp.concatenate([object_bf, object_bf[:, :P_SIZE, :]], axis=1)
    wrapped = jnp.concatenate([wrapped, wrapped[:, :, :P_SIZE]], axis=2)
    anchor = jnp.int32(0)
    row_slots = N_COL * SLOT_DEV

    def add_slot(counter, accumulated):
        counter = jnp.asarray(counter).astype(jnp.int32)
        tile_row = counter // row_slots
        slot_col = counter % row_slots
        tile_col = slot_col // SLOT_DEV
        slot_index = slot_col % SLOT_DEV
        row_at = (tile_row * P_SIZE + offset_y[tile_row, slot_col]).astype(jnp.int32)
        col_at = (tile_col * P_SIZE + offset_x[tile_row, slot_col]).astype(jnp.int32)

        def process(current):
            patch_tile = lax.dynamic_slice(wrapped, (anchor, row_at, col_at), (2, P_SIZE, P_SIZE))
            half_spec = spectrum_rows(patch_tile, probe_re, probe_im, cos_table, sin_table)
            partial_back = correct_rows(half_spec, amplitude[tile_row, slot_col], cos_table, sin_table)
            update = object_term(partial_back, probe_re, probe_im, cos_table, sin_table)
            window = lax.dynamic_slice(current, (anchor, row_at, col_at), (2, P_SIZE, P_SIZE))
            return lax.dynamic_update_slice(current, window + update, (anchor, row_at, col_at))

        def unchanged(current):
            return current
        return lax.cond(slot_index < counts[tile_row, tile_col], process, unchanged, accumulated)
    accumulated = lax.fori_loop(0, N_ROW * row_slots, add_slot, jnp.zeros((2, NY + P_SIZE, NX + P_SIZE), jnp.float32))
    intersection = accumulated[:, :NY, :NX]
    intersection = intersection.at[:, :P_SIZE, :].add(accumulated[:, NY:, :NX])
    intersection = intersection.at[:, :, :P_SIZE].add(accumulated[:, :NY, NX:])
    intersection = intersection.at[:, :P_SIZE, :P_SIZE].add(accumulated[:, NY:, NX:])
    half_step = jnp.stack([obj_re, obj_im]) + step_size / probe_power * intersection
    shifted = jnp.roll(half_step, (-1, -1), axis=(1, 2))
    cleaned = 0.5 * (haar_clean(half_step) + jnp.roll(haar_clean(shifted), (1, 1), axis=(1, 2)))
    return (cleaned[0], cleaned[1])
```

```python
import functools
import math

import jax
import jax.numpy as jnp
import numpy as np
from jax import lax
from jax.experimental import pallas as pl
from jax.experimental.pallas import tpu as pltpu
from jax.sharding import PartitionSpec as P

modulus_floor = 0.5
shrink_level = 0.2
step_size = 0.5
epsilon = 1e-05
LANES = 128


def transform_tables(side):
    quarter, half = side // 4, side // 2
    bf16 = jnp.bfloat16

    def cos_sin(rows, cols):
        angle = (rows[:, None] * cols[None, :] % side) * (2.0 * math.pi / side)
        norm = 1.0 / math.sqrt(side)
        return np.cos(angle) * norm, -np.sin(angle) * norm

    base = np.arange(quarter)
    grouped = np.concatenate([base[c::4] for c in range(4)])
    rows_in, rows_out = [], []
    for c in range(4):
        members = 4 * base + c
        co, si = cos_sin(grouped, members)
        rows_in.append(np.block([[co, -si], [si, co]]))
        co, si = cos_sin(base, members)
        rows_out.append(np.block([[co, si], [-si, co]]))
    frequency = np.concatenate([np.arange(0, half, 2), np.arange(1, half, 2)])
    mirrored = (side - frequency) % side
    mirrored[0] = half
    every = np.arange(side)
    co, si = cos_sin(every, frequency)
    co[:, 0] = np.where(every % 2 == 0, co[:, 0], 0.0)
    si[:, 0] = np.where(every % 2 == 1, 1.0 / math.sqrt(side), 0.0)
    cols_in = np.concatenate([co, si], axis=1)
    cols_out = []
    for part in range(2):
        run = slice(part * quarter, (part + 1) * quarter)
        members = np.concatenate([frequency[run], mirrored[run]])
        co, si = cos_sin(members, np.arange(half))
        cols_out.append(np.block([[co, -si], [si, co]]))
    order = np.concatenate([frequency, mirrored])
    pick = np.zeros((side, side))
    pick[order, every] = 1.0
    as_bf16 = lambda table: jnp.asarray(np.asarray(table, np.float32)).astype(bf16)
    return tuple(
        np.asarray(np.asarray(table, np.float32), dtype=bf16)
        for table in (np.stack(rows_in), cols_in, np.stack(cols_out), np.stack(rows_out), pick)
    )


def dot(left_op, right_op):
    return jnp.dot(left_op, right_op, preferred_element_type=jnp.float32)


def slots_kernel(
    side,
    count_ref,
    oy_ref,
    ox_ref,
    own_re,
    own_im,
    right_ref,
    below_ref,
    diag_ref,
    probe_re,
    probe_im,
    amp_ref,
    rows_in,
    cols_in,
    cols_out,
    rows_out,
    pick,
    own_out,
    right_out,
    below_out,
    diag_out,
    region,
    sums,
    probe,
    exits,
    wide,
    half,
    delta,
    back,
    amp,
):
    quarter, chunks = side // 4, side // LANES
    f32, bf16 = jnp.float32, jnp.bfloat16
    tiles = ((own_re, own_im), right_ref, below_ref, diag_ref)

    for p in range(2):
        for a in range(chunks):
            lanes = slice(a * LANES, (a + 1) * LANES)
            own = (own_re, own_im)[p]
            region[p, a, :side, :] = own[:, lanes].astype(bf16).astype(f32)
            region[p, chunks + a, :side, :] = right_ref[p, :, lanes].astype(f32)
            region[p, a, side:, :] = below_ref[p, :, lanes].astype(f32)
            region[p, chunks + a, side:, :] = diag_ref[p, :, lanes].astype(f32)
            probe[p, a] = (probe_re, probe_im)[p][:, lanes]
    sums[...] = jnp.zeros_like(sums)

    lane = lax.broadcasted_iota(jnp.int32, (1, LANES), 1)

    def one_slot(s, carry):
        oy = oy_ref[0, s]
        ox = ox_ref[0, s]
        q = ox // LANES
        b = ox % LANES
        inward = (LANES - b) % LANES
        keep = lane < LANES - b
        placed = lane >= b

        for c in range(4):
            rows = pl.ds(oy + c, quarter, stride=4)
            before = None
            for a in range(chunks + 1):
                now = [pltpu.roll(region[p, q + a, rows, :], inward, axis=1) for p in range(2)]
                if a > 0:
                    o_re, o_im = (jnp.where(keep, before[p], now[p]) for p in range(2))
                    mine = pl.ds(c, quarter, stride=4)
                    p_re, p_im = probe[0, a - 1, mine, :], probe[1, a - 1, mine, :]
                    lanes = slice((a - 1) * LANES, a * LANES)
                    exits[c, :quarter, lanes] = (p_re * o_re - p_im * o_im).astype(bf16)
                    exits[c, quarter:, lanes] = (p_re * o_im + p_im * o_re).astype(bf16)
                before = now
        for c in range(4):
            wide[c] = dot(rows_in[c], exits[c])
        step = quarter // 4
        for cc in range(4):
            for a in range(chunks):
                lanes = slice(a * LANES, (a + 1) * LANES)
                re = [wide[c, cc * step : (cc + 1) * step, lanes] for c in range(4)]
                im = [wide[c, quarter + cc * step : quarter + (cc + 1) * step, lanes] for c in range(4)]
                er, ei, fr, fi = re[0] + re[2], im[0] + im[2], re[0] - re[2], im[0] - im[2]
                gr, gi, hr, hi = re[1] + re[3], im[1] + im[3], re[1] - re[3], im[1] - im[3]
                outs = (
                    (er + gr, ei + gi),
                    (fr + hi, fi - hr),
                    (er - gr, ei - gi),
                    (fr - hi, fi + hr),
                )
                for m, (o_re, o_im) in enumerate(outs):
                    half[cc, m * step : (m + 1) * step, lanes] = o_re.astype(bf16)
                    half[cc, quarter + m * step : quarter + (m + 1) * step, lanes] = o_im.astype(bf16)

        ordered = dot(amp_ref[0, s], pick[...])
        for a in range(chunks):
            amp[a] = ordered[:, a * LANES : (a + 1) * LANES]

        for cc in range(4):
            wide[cc] = dot(half[cc], cols_in[...])
        mid = chunks // 2
        for cc in range(4):
            for part in range(mid):
                lo = slice(part * LANES, (part + 1) * LANES)
                hi = slice((mid + part) * LANES, (mid + part + 1) * LANES)
                p1, p3 = wide[cc, :quarter, lo], wide[cc, :quarter, hi]
                p4, p2 = wide[cc, quarter:, lo], wide[cc, quarter:, hi]
                if part == 0:
                    p2, p3 = jnp.where(lane == 0, -p3, p2), jnp.where(lane == 0, p2, p3)
                for sign in range(2):
                    s_re = p1 - p2 if sign == 0 else p1 + p2
                    s_im = p4 + p3 if sign == 0 else p4 - p3
                    measured = amp[sign * mid + part, pl.ds(cc, quarter, stride=4), :]
                    inverse = jnp.minimum(lax.rsqrt(s_re * s_re + s_im * s_im), 1.0 / modulus_floor)
                    factor = measured * inverse - 1.0
                    rows = slice(cc * quarter, (cc + 1) * quarter)
                    for k, value in ((sign, s_re), (2 + sign, s_im)):
                        delta[part, rows, k * LANES : (k + 1) * LANES] = (value * factor).astype(bf16)

        for part in range(2):
            for r in range(2):
                wide[2 * part + r] = dot(delta[part, r * side // 2 : (r + 1) * side // 2, :], cols_out[part])
        for cc in range(4):
            for k in range(2):
                for a in range(mid):
                    lanes = slice((k * mid + a) * LANES, (k * mid + a + 1) * LANES)
                    rows = slice((cc % 2) * quarter, (cc % 2 + 1) * quarter)
                    even, odd = wide[cc // 2, rows, lanes], wide[2 + cc // 2, rows, lanes]
                    put = slice(k * quarter, (k + 1) * quarter)
                    back[cc, put, a * LANES : (a + 1) * LANES] = (even + odd).astype(bf16)
                    back[cc, put, (mid + a) * LANES : (mid + a + 1) * LANES] = (even - odd).astype(bf16)

        for c in range(4):
            wide[c] = dot(rows_out[c], back[c])
        rows_at = 16
        for r in range(quarter // rows_at):
            before = [None] * 8
            for a in range(chunks + 1):
                now = [None] * 8
                if a < chunks:
                    lanes = slice(a * LANES, (a + 1) * LANES)
                    at = r * rows_at
                    re = [wide[c, at : at + rows_at, lanes] for c in range(4)]
                    im = [wide[c, quarter + at : quarter + at + rows_at, lanes] for c in range(4)]
                    er, ei, fr, fi = re[0] + re[2], im[0] + im[2], re[0] - re[2], im[0] - im[2]
                    gr, gi, hr, hi = re[1] + re[3], im[1] + im[3], re[1] - re[3], im[1] - im[3]
                    outs = (
                        (er + gr, ei + gi),
                        (fr - hi, fi + hr),
                        (er - gr, ei - gi),
                        (fr + hi, fi - hr),
                    )
                    for m, (w_re, w_im) in enumerate(outs):
                        mine = slice(m * quarter + at, m * quarter + at + rows_at)
                        p_re, p_im = probe[0, a, mine, :], probe[1, a, mine, :]
                        now[2 * m] = pltpu.roll(p_re * w_re + p_im * w_im, b, axis=1)
                        now[2 * m + 1] = pltpu.roll(p_re * w_im - p_im * w_re, b, axis=1)
                for k in range(8):
                    one = jnp.zeros((rows_at, LANES), f32) if now[k] is None else now[k]
                    two = jnp.zeros((rows_at, LANES), f32) if before[k] is None else before[k]
                    rows = pl.ds(oy + (k // 2) * quarter + r * rows_at, rows_at)
                    sums[k % 2, q + a, rows, :] += jnp.where(placed, one, two)
                before = now
        return carry

    lax.fori_loop(0, count_ref[0, 0], one_slot, 0)

    for p in range(2):
        for a in range(chunks):
            lanes = slice(a * LANES, (a + 1) * LANES)
            own_out[p, :, lanes] = sums[p, a, :side, :]
            right_out[p, :, lanes] = sums[p, chunks + a, :side, :].astype(bf16)
            below_out[p, :, lanes] = sums[p, a, side:, :].astype(below_out.dtype)
            diag_out[p, :, lanes] = sums[p, chunks + a, side:, :].astype(bf16)


def run_slots(counts, offset_y, offset_x, obj_re, obj_im, right, below, diag, probe_re, probe_im, amplitude):
    side = probe_re.shape[0]
    chunks, quarter = side // LANES, side // 4
    f32, bf16 = jnp.float32, jnp.bfloat16
    tables = transform_tables(side)
    smem = pl.BlockSpec(memory_space=pltpu.SMEM)
    vmem = pl.BlockSpec(memory_space=pltpu.VMEM)
    tile = lambda kind: jax.ShapeDtypeStruct((2, side, side), kind)
    return pl.pallas_call(
        functools.partial(slots_kernel, side),
        out_shape=(tile(f32), tile(bf16), tile(f32), tile(bf16)),
        in_specs=[smem] * 3 + [vmem] * 13,
        out_specs=[vmem] * 4,
        scratch_shapes=[
            pltpu.VMEM((2, 2 * chunks, 2 * side, LANES), f32),
            pltpu.VMEM((2, 2 * chunks, 2 * side, LANES), f32),
            pltpu.VMEM((2, chunks, side, LANES), f32),
            pltpu.VMEM((4, 2 * quarter, side), bf16),
            pltpu.VMEM((4, 2 * quarter, side), f32),
            pltpu.VMEM((4, 2 * quarter, side), bf16),
            pltpu.VMEM((2, side, side), bf16),
            pltpu.VMEM((4, 2 * quarter, side), bf16),
            pltpu.VMEM((chunks, side, LANES), f32),
        ],
        name="slots",
    )(counts, offset_y, offset_x, obj_re, obj_im, right, below, diag, probe_re, probe_im, amplitude, *tables)


def haar_kernel(hs_ref, top_ref, bottom_ref, left_ref, right_ref, out_re, out_im):
    side = hs_ref.shape[1]
    chunks = side // LANES
    block = 64
    level = shrink_level
    soft = lambda t: t - jnp.clip(t, -level, level)
    lane = lax.broadcasted_iota(jnp.int32, (1, LANES), 1)
    row = lax.broadcasted_iota(jnp.int32, (block, 1), 0)
    even_lane, even_row = lane % 2 == 0, row % 2 == 0

    def finish(total, gap, total_x, gap_x):
        coarse = 0.5 * (total + total_x)
        across = soft(0.5 * (total - total_x))
        downward = soft(0.5 * (gap + gap_x))
        diagonal = soft(0.5 * (gap - gap_x))
        return 0.5 * (coarse + across + downward + diagonal)

    for p in range(2):
        out = (out_re, out_im)[p]
        for r in range(side // block):
            at = r * block
            sums_of, gaps_of, plain = [], [], []
            for a in range(chunks):
                lanes = slice(a * LANES, (a + 1) * LANES)
                x = hs_ref[p, at : at + block, lanes]
                down = pltpu.roll(x, block - 1, axis=0)
                up = pltpu.roll(x, 1, axis=0)
                mate = jnp.where(even_row, down, up)
                total, gap = x + mate, x - mate
                mirror = lambda t: jnp.where(even_lane, pltpu.roll(t, LANES - 1, axis=1), pltpu.roll(t, 1, axis=1))
                plain.append(finish(total, gap, mirror(total), mirror(gap)))
                after = hs_ref[p, at + block : at + block + 1, lanes] if at + block < side else bottom_ref[p, :, lanes]
                ahead = hs_ref[p, at - 1 : at, lanes] if at > 0 else top_ref[p, :, lanes]
                down = jnp.where(row == block - 1, after, down)
                up = jnp.where(row == 0, ahead, up)
                mate = jnp.where(even_row, up, down)
                sums_of.append(x + mate)
                gaps_of.append(x - mate)
            rows = slice(at, at + block)

            def beside(ref):
                x, up, down = ref[p, 0, rows, :], ref[p, 1, rows, :], ref[p, 2, rows, :]
                mate = jnp.where(even_row, up, down)
                return x + mate, x - mate

            left, right = beside(left_ref), beside(right_ref)
            turned = [[(pltpu.roll(t, 1, axis=1), pltpu.roll(t, LANES - 1, axis=1)) for t in both] for both in (sums_of, gaps_of)]
            for a in range(chunks):
                other = []
                for k in range(2):
                    from_left = turned[k][a - 1][0] if a > 0 else left[k]
                    from_right = turned[k][a + 1][1] if a + 1 < chunks else right[k]
                    to_left = jnp.where(lane == 0, from_left, turned[k][a][0])
                    to_right = jnp.where(lane == LANES - 1, from_right, turned[k][a][1])
                    other.append(jnp.where(even_lane, to_left, to_right))
                moved = finish(sums_of[a], gaps_of[a], other[0], other[1])
                out[rows, a * LANES : (a + 1) * LANES] = 0.5 * (plain[a] + moved)


def run_haar(hs, top, bottom, left, right):
    side = hs.shape[1]
    vmem = pl.BlockSpec(memory_space=pltpu.VMEM)
    tile = jax.ShapeDtypeStruct((side, side), jnp.float32)
    return pl.pallas_call(
        haar_kernel,
        out_shape=(tile, tile),
        in_specs=[vmem] * 5,
        out_specs=[vmem] * 2,
        name="haar",
    )(hs, top, bottom, left, right)


def shifted(value, axis, steps):
    count = lax.axis_size(axis)
    return lax.ppermute(value, axis, [(i, (i + steps) % count) for i in range(count)])


def body(obj_re, obj_im, probe_re, probe_im, amplitude, offset_y, offset_x, counts):
    f32, bf16 = jnp.float32, jnp.bfloat16
    side = probe_re.shape[0]
    probe_power = jnp.mean(probe_re * probe_re + probe_im * probe_im) + epsilon
    own = jnp.stack([obj_re, obj_im]).astype(bf16)
    below = shifted(own, "row", -1)
    right = shifted(own, "col", -1)
    diag = shifted(below, "col", -1)
    own_sum, right_sum, below_sum, diag_sum = run_slots(
        counts, offset_y, offset_x, obj_re, obj_im, right, below, diag, probe_re, probe_im, amplitude
    )
    diag_in = shifted(diag_sum, "col", 1)
    right_in = shifted(right_sum, "col", 1)
    below_in = shifted((below_sum + diag_in.astype(f32)).astype(bf16), "row", 1)
    total = own_sum + right_in.astype(f32) + below_in.astype(f32)
    half_step = jnp.stack([obj_re, obj_im]) + step_size / probe_power * total
    top = shifted(half_step[:, -1:, :], "row", 1)
    bottom = shifted(half_step[:, :1, :], "row", -1)
    edges = jnp.concatenate([top, half_step[:, :, :], bottom], axis=1)
    left = shifted(edges[:, :, -1], "col", 1)
    right = shifted(edges[:, :, 0], "col", -1)

    def three(column):
        return jnp.stack([column[:, 1:-1], column[:, :-2], column[:, 2:]], axis=1)[..., None]

    return run_haar(half_step, top, bottom, three(left), three(right))


def solution(mesh):
    split = P("row", "col")
    return jax.shard_map(
        body,
        mesh=mesh,
        in_specs=(split, split, P(), P(), P("row", "col", None, None), split, split, split),
        out_specs=(split, split),
        check_vma=False,
    )
```

```python
import functools
import math

import jax
import jax.numpy as jnp
import numpy as np
from jax import lax
from jax.experimental import pallas as pl
from jax.experimental.pallas import tpu as pltpu
from jax.sharding import PartitionSpec as P

modulus_floor = 0.5
shrink_level = 0.2
step_size = 0.5
epsilon = 1e-05
LANES = 128


def transform_tables(side):
    quarter, half = side // 4, side // 2
    bf16 = jnp.bfloat16

    def cos_sin(rows, cols):
        angle = (rows[:, None] * cols[None, :] % side) * (2.0 * math.pi / side)
        norm = 1.0 / math.sqrt(side)
        return np.cos(angle) * norm, -np.sin(angle) * norm

    base = np.arange(quarter)
    grouped = np.concatenate([base[c::4] for c in range(4)])
    rows_in, rows_out = [], []
    for c in range(4):
        members = 4 * base + c
        co, si = cos_sin(grouped, members)
        rows_in.append(np.block([[co, -si], [si, co]]))
        co, si = cos_sin(base, members)
        rows_out.append(np.block([[co, si], [-si, co]]))
    frequency = np.concatenate([np.arange(0, half, 2), np.arange(1, half, 2)])
    mirrored = (side - frequency) % side
    mirrored[0] = half
    every = np.arange(side)
    co, si = cos_sin(every, frequency)
    co[:, 0] = np.where(every % 2 == 0, co[:, 0], 0.0)
    si[:, 0] = np.where(every % 2 == 1, 1.0 / math.sqrt(side), 0.0)
    cols_in = np.concatenate([co, si], axis=1)
    cols_out = []
    for part in range(2):
        run = slice(part * quarter, (part + 1) * quarter)
        members = np.concatenate([frequency[run], mirrored[run]])
        co, si = cos_sin(members, np.arange(half))
        cols_out.append(np.block([[co, -si], [si, co]]))
    order = np.concatenate([frequency, mirrored])
    pick = np.zeros((side, side))
    pick[order, every] = 1.0
    as_bf16 = lambda table: jnp.asarray(np.asarray(table, np.float32)).astype(bf16)
    return tuple(
        np.asarray(np.asarray(table, np.float32), dtype=bf16)
        for table in (np.stack(rows_in), cols_in, np.stack(cols_out), np.stack(rows_out), pick)
    )


def dot(left_op, right_op):
    return jnp.dot(left_op, right_op, preferred_element_type=jnp.float32)


def slots_kernel(side, in_parts, out_parts, *refs):
    refs = list(refs)

    def take(count):
        taken = refs[:count]
        del refs[:count]
        return taken

    count_ref, oy_ref, ox_ref, scale_ref, own_re, own_im, right_ref = take(7)
    below_refs, diag_refs = take(len(in_parts)), take(len(in_parts))
    probe_re, probe_im, amp_ref = take(3)
    rows_in, cols_in, cols_out, rows_out, pick = take(5)
    own_out, right_out, edge_out = take(3)
    below_outs, diag_outs = take(len(out_parts)), take(len(out_parts))
    region, sums, probe, exits, wide, half, delta, back, amp = refs
    quarter, chunks = side // 4, side // LANES
    f32, bf16 = jnp.float32, jnp.bfloat16

    for p in range(2):
        for a in range(chunks):
            lanes = slice(a * LANES, (a + 1) * LANES)
            own = (own_re, own_im)[p]
            region[p, a, :side, :] = own[:, lanes].astype(bf16).astype(f32)
            region[p, chunks + a, :side, :] = right_ref[p, :, lanes].astype(f32)
            at = side
            for rows, below_ref, diag_ref in zip(in_parts, below_refs, diag_refs):
                region[p, a, at : at + rows, :] = below_ref[p, :, lanes].astype(f32)
                region[p, chunks + a, at : at + rows, :] = diag_ref[p, :, lanes].astype(f32)
                at += rows
            probe[p, a] = (probe_re, probe_im)[p][:, lanes]
    sums[...] = jnp.zeros_like(sums)

    lane = lax.broadcasted_iota(jnp.int32, (1, LANES), 1)

    def one_slot(s, carry):
        oy = oy_ref[0, s]
        ox = ox_ref[0, s]
        q = ox // LANES
        b = ox % LANES
        inward = (LANES - b) % LANES
        keep = lane < LANES - b
        placed = lane >= b

        for c in range(4):
            rows = pl.ds(oy + c, quarter, stride=4)
            before = None
            for a in range(chunks + 1):
                now = [pltpu.roll(region[p, q + a, rows, :], inward, axis=1) for p in range(2)]
                if a > 0:
                    o_re, o_im = (jnp.where(keep, before[p], now[p]) for p in range(2))
                    mine = pl.ds(c, quarter, stride=4)
                    p_re, p_im = probe[0, a - 1, mine, :], probe[1, a - 1, mine, :]
                    lanes = slice((a - 1) * LANES, a * LANES)
                    exits[c, :quarter, lanes] = (p_re * o_re - p_im * o_im).astype(bf16)
                    exits[c, quarter:, lanes] = (p_re * o_im + p_im * o_re).astype(bf16)
                before = now
        for c in range(4):
            wide[c] = dot(rows_in[c], exits[c])
        step = quarter // 4
        for cc in range(4):
            for a in range(chunks):
                lanes = slice(a * LANES, (a + 1) * LANES)
                re = [wide[c, cc * step : (cc + 1) * step, lanes] for c in range(4)]
                im = [wide[c, quarter + cc * step : quarter + (cc + 1) * step, lanes] for c in range(4)]
                er, ei, fr, fi = re[0] + re[2], im[0] + im[2], re[0] - re[2], im[0] - im[2]
                gr, gi, hr, hi = re[1] + re[3], im[1] + im[3], re[1] - re[3], im[1] - im[3]
                outs = (
                    (er + gr, ei + gi),
                    (fr + hi, fi - hr),
                    (er - gr, ei - gi),
                    (fr - hi, fi + hr),
                )
                for m, (o_re, o_im) in enumerate(outs):
                    half[cc, m * step : (m + 1) * step, lanes] = o_re.astype(bf16)
                    half[cc, quarter + m * step : quarter + (m + 1) * step, lanes] = o_im.astype(bf16)

        ordered = dot(amp_ref[0, s], pick[...])
        for a in range(chunks):
            amp[a] = ordered[:, a * LANES : (a + 1) * LANES]

        for cc in range(4):
            wide[cc] = dot(half[cc], cols_in[...])
        mid = chunks // 2
        for cc in range(4):
            for part in range(mid):
                lo = slice(part * LANES, (part + 1) * LANES)
                hi = slice((mid + part) * LANES, (mid + part + 1) * LANES)
                p1, p3 = wide[cc, :quarter, lo], wide[cc, :quarter, hi]
                p4, p2 = wide[cc, quarter:, lo], wide[cc, quarter:, hi]
                if part == 0:
                    p2, p3 = jnp.where(lane == 0, -p3, p2), jnp.where(lane == 0, p2, p3)
                for sign in range(2):
                    s_re = p1 - p2 if sign == 0 else p1 + p2
                    s_im = p4 + p3 if sign == 0 else p4 - p3
                    measured = amp[sign * mid + part, pl.ds(cc, quarter, stride=4), :]
                    inverse = jnp.minimum(lax.rsqrt(s_re * s_re + s_im * s_im), 1.0 / modulus_floor)
                    factor = measured * inverse - 1.0
                    rows = slice(cc * quarter, (cc + 1) * quarter)
                    for k, value in ((sign, s_re), (2 + sign, s_im)):
                        delta[part, rows, k * LANES : (k + 1) * LANES] = (value * factor).astype(bf16)

        for part in range(2):
            for r in range(2):
                wide[2 * part + r] = dot(delta[part, r * side // 2 : (r + 1) * side // 2, :], cols_out[part])
        for cc in range(4):
            for k in range(2):
                for a in range(mid):
                    lanes = slice((k * mid + a) * LANES, (k * mid + a + 1) * LANES)
                    rows = slice((cc % 2) * quarter, (cc % 2 + 1) * quarter)
                    even, odd = wide[cc // 2, rows, lanes], wide[2 + cc // 2, rows, lanes]
                    put = slice(k * quarter, (k + 1) * quarter)
                    back[cc, put, a * LANES : (a + 1) * LANES] = (even + odd).astype(bf16)
                    back[cc, put, (mid + a) * LANES : (mid + a + 1) * LANES] = (even - odd).astype(bf16)

        for c in range(4):
            wide[c] = dot(rows_out[c], back[c])
        rows_at = 16
        for r in range(quarter // rows_at):
            before = [None] * 8
            for a in range(chunks + 1):
                now = [None] * 8
                if a < chunks:
                    lanes = slice(a * LANES, (a + 1) * LANES)
                    at = r * rows_at
                    re = [wide[c, at : at + rows_at, lanes] for c in range(4)]
                    im = [wide[c, quarter + at : quarter + at + rows_at, lanes] for c in range(4)]
                    er, ei, fr, fi = re[0] + re[2], im[0] + im[2], re[0] - re[2], im[0] - im[2]
                    gr, gi, hr, hi = re[1] + re[3], im[1] + im[3], re[1] - re[3], im[1] - im[3]
                    outs = (
                        (er + gr, ei + gi),
                        (fr - hi, fi + hr),
                        (er - gr, ei - gi),
                        (fr + hi, fi - hr),
                    )
                    for m, (w_re, w_im) in enumerate(outs):
                        mine = slice(m * quarter + at, m * quarter + at + rows_at)
                        p_re, p_im = probe[0, a, mine, :], probe[1, a, mine, :]
                        now[2 * m] = pltpu.roll(p_re * w_re + p_im * w_im, b, axis=1)
                        now[2 * m + 1] = pltpu.roll(p_re * w_im - p_im * w_re, b, axis=1)
                for k in range(8):
                    one = jnp.zeros((rows_at, LANES), f32) if now[k] is None else now[k]
                    two = jnp.zeros((rows_at, LANES), f32) if before[k] is None else before[k]
                    rows = pl.ds(oy + (k // 2) * quarter + r * rows_at, rows_at)
                    sums[k % 2, q + a, rows, :] += jnp.where(placed, one, two)
                before = now
        return carry

    lax.fori_loop(0, count_ref[0, 0], one_slot, 0)

    scale = scale_ref[0, 0]
    for p in range(2):
        own = (own_re, own_im)[p]
        for a in range(chunks):
            lanes = slice(a * LANES, (a + 1) * LANES)
            right_out[p, :, lanes] = (scale * sums[p, chunks + a, :side, :]).astype(bf16)
            own_out[p, :, lanes] = own[:, lanes] + scale * sums[p, a, :side, :]
            at = side
            for rows, below_out, diag_out in zip(out_parts, below_outs, diag_outs):
                below_out[p, :, lanes] = scale * sums[p, a, at : at + rows, :]
                diag_out[p, :, lanes] = (scale * sums[p, chunks + a, at : at + rows, :]).astype(bf16)
                at += rows
        for k, (a, at) in enumerate(((0, 0), (chunks - 1, LANES - 1), (chunks, 0), (2 * chunks - 1, LANES - 1))):
            for r in range(2 * side // LANES):
                cells = scale * sums[p, a, r * LANES : (r + 1) * LANES, :]
                if k < 2 and r < chunks:
                    cells += own[r * LANES : (r + 1) * LANES, a * LANES : (a + 1) * LANES]
                edge_out[p, k : k + 1, r * LANES : (r + 1) * LANES] = cells.T[at : at + 1, :]


def run_slots(counts, offset_y, offset_x, scale, obj_re, obj_im, right, below, diag, probe_re, probe_im, amplitude, out_parts):
    side = probe_re.shape[0]
    chunks, quarter = side // LANES, side // 4
    f32, bf16 = jnp.float32, jnp.bfloat16
    tables = transform_tables(side)
    in_parts = [part.shape[1] for part in below]
    smem = pl.BlockSpec(memory_space=pltpu.SMEM)
    vmem = pl.BlockSpec(memory_space=pltpu.VMEM)
    tile = lambda rows, kind: jax.ShapeDtypeStruct((2, rows, side), kind)
    outs = [tile(side, f32), tile(side, bf16), jax.ShapeDtypeStruct((2, 4, 2 * side), f32)]
    outs += [tile(rows, f32) for rows in out_parts] + [tile(rows, bf16) for rows in out_parts]
    results = pl.pallas_call(
        functools.partial(slots_kernel, side, in_parts, out_parts),
        out_shape=outs,
        in_specs=[smem] * 4 + [vmem] * (11 + 2 * len(in_parts)),
        out_specs=[vmem] * len(outs),
        scratch_shapes=[
            pltpu.VMEM((2, 2 * chunks, 2 * side, LANES), f32),
            pltpu.VMEM((2, 2 * chunks, 2 * side, LANES), f32),
            pltpu.VMEM((2, chunks, side, LANES), f32),
            pltpu.VMEM((4, 2 * quarter, side), bf16),
            pltpu.VMEM((4, 2 * quarter, side), f32),
            pltpu.VMEM((4, 2 * quarter, side), bf16),
            pltpu.VMEM((2, side, side), bf16),
            pltpu.VMEM((4, 2 * quarter, side), bf16),
            pltpu.VMEM((chunks, side, LANES), f32),
        ],
        compiler_params=pltpu.CompilerParams(vmem_limit_bytes=46 * 2**20),
        name="slots",
    )(counts, offset_y, offset_x, scale, obj_re, obj_im, right, *below, *diag, probe_re, probe_im, amplitude, *tables)
    parts = len(out_parts)
    return results[0], results[1], results[2], results[3 : 3 + parts], results[3 + parts :]


def finish_kernel(parts, *refs):
    own_ref, right_ref = refs[:2]
    below_refs = refs[2 : 2 + len(parts)]
    top_ref, bottom_ref, ring_ref, out_re, out_im, cells, spill, result = refs[2 + len(parts) :]
    side = own_ref.shape[1]
    chunks = side // LANES
    f32 = jnp.float32
    pad, count = 16, 8
    ring = ring_ref[...].T
    for p in range(2):
        for a in range(chunks):
            lanes = slice(a * LANES, (a + 1) * LANES)
            at = 0
            for rows, below_ref in zip(parts, below_refs):
                mine = slice(at, at + rows)
                cells[p, a + 1, pad + at : pad + at + rows, :] = (
                    own_ref[p, mine, lanes] + right_ref[p, mine, lanes].astype(f32) + below_ref[p, :, lanes].astype(f32)
                )
                at += rows
        for k in range(2):
            beside = jnp.broadcast_to(ring[:, 2 * k + p : 2 * k + p + 1], (side, LANES))
            cells[p, k * (chunks + 1), pad : pad + side, :] = beside
        for a in range(chunks + 2):
            cells[p, a, pad - 1 : pad, :] = top_ref[p, a : a + 1, :]
            cells[p, a, pad + side : pad + side + 1, :] = bottom_ref[p, a : a + 1, :]

    bound = 2.0 * shrink_level
    lane = lax.broadcasted_iota(jnp.int32, (count, LANES), 1)
    even, first, last = lane % 2 == 0, lane == 0, lane == LANES - 1
    cut = lambda t: jnp.clip(t, -bound, bound)
    later = lambda t: pltpu.roll(t, 1, axis=1)
    sooner = lambda t: pltpu.roll(t, LANES - 1, axis=1)

    def clips(total, gap, total_x, gap_x):
        side_by_side = cut(total - total_x)
        other = cut(gap + gap_x) + cut(gap - gap_x)
        return side_by_side + other, side_by_side - other

    def moved(p, at):
        upper = pl.ds(pad + 1 + 2 * at, count, stride=2)
        lower = pl.ds(pad + 2 + 2 * at, count, stride=2)
        high = [cells[p, a, upper, :] for a in range(chunks + 2)]
        low = [cells[p, a, lower, :] for a in range(chunks + 2)]
        fields = [[h + w for h, w in zip(high, low)], [h - w for h, w in zip(high, low)]]
        turned = []
        for field in fields:
            right_of = [later(field[a]) for a in range(chunks + 1)]
            left_of = [sooner(field[a]) for a in range(1, chunks + 2)]
            turned.append(
                [
                    jnp.where(
                        even,
                        jnp.where(first, right_of[a - 1], right_of[a]),
                        jnp.where(last, left_of[a], left_of[a - 1]),
                    )
                    for a in range(1, chunks + 1)
                ]
            )
        return [clips(fields[0][a + 1], fields[1][a + 1], turned[0][a], turned[1][a]) for a in range(chunks)]

    for p in range(2):
        for a, (_, below_one) in enumerate(moved(p, -count)):
            spill[p, a, 1 : 1 + count, :] = below_one

    def block(i, carry):
        at = pl.multiple_of(i * count, count)
        for p in range(2):
            shifted_clips = moved(p, at)
            for a in range(chunks):
                upper = pl.ds(pad + 2 * at, count, stride=2)
                lower = pl.ds(pad + 1 + 2 * at, count, stride=2)
                high, low = cells[p, a + 1, upper, :], cells[p, a + 1, lower, :]
                total, gap = high + low, high - low
                total_x = jnp.where(even, sooner(total), later(total))
                gap_x = jnp.where(even, sooner(gap), later(gap))
                top_clip, low_clip = clips(total, gap, total_x, gap_x)
                spill[p, a, pl.ds(at + count + 1, count), :] = shifted_clips[a][1]
                top_clip += spill[p, a, pl.ds(at + count, count), :]
                low_clip += shifted_clips[a][0]
                result[p, a, pl.ds(2 * at, count, stride=2), :] = high - 0.125 * top_clip
                result[p, a, pl.ds(2 * at + 1, count, stride=2), :] = low - 0.125 * low_clip
            for a in range(chunks):
                mine = pl.ds(2 * at, 2 * count)
                (out_re, out_im)[p][mine, a * LANES : (a + 1) * LANES] = result[p, a, mine, :]
        return carry

    lax.fori_loop(0, side // (2 * count), block, 0)


def run_finish(own, right, below, top, bottom, ring):
    side = own.shape[1]
    chunks = side // LANES
    f32 = jnp.float32
    vmem = pl.BlockSpec(memory_space=pltpu.VMEM)
    tile = jax.ShapeDtypeStruct((side, side), f32)
    parts = [part.shape[1] for part in below]
    return pl.pallas_call(
        functools.partial(finish_kernel, parts),
        out_shape=(tile, tile),
        in_specs=[vmem] * (5 + len(parts)),
        out_specs=[vmem] * 2,
        scratch_shapes=[
            pltpu.VMEM((2, chunks + 2, side + 32, LANES), f32),
            pltpu.VMEM((2, chunks, side // 2 + 16, LANES), f32),
            pltpu.VMEM((2, chunks, side, LANES), f32),
        ],
        compiler_params=pltpu.CompilerParams(vmem_limit_bytes=20 * 2**20),
        name="finish",
    )(own, right, *below, top, bottom, ring)


def shifted(value, axis, steps):
    count = lax.axis_size(axis)
    return lax.ppermute(value, axis, [(i, (i + steps) % count) for i in range(count)])


def parts_of(side, weights):
    unit = side // 32
    sizes = [unit * weight for weight in weights]
    assert sum(sizes) == side and unit % 16 == 0
    return sizes


def split_rows(value, sizes):
    ends = np.cumsum(sizes)
    return [value[:, end - size : end] for end, size in zip(ends, sizes)]


def body(obj_re, obj_im, probe_re, probe_im, amplitude, offset_y, offset_x, counts):
    f32, bf16 = jnp.float32, jnp.bfloat16
    side = probe_re.shape[0]
    in_parts, out_parts = parts_of(side, (16, 10, 6)), parts_of(side, (4, 12, 16))
    probe_power = jnp.mean(probe_re * probe_re + probe_im * probe_im) + epsilon
    scale = (step_size / probe_power).reshape(1, 1)
    own = jnp.stack([obj_re, obj_im])
    pieces = [piece.astype(bf16) for piece in split_rows(own, in_parts)]
    below = [shifted(piece, "row", -1) for piece in pieces]
    right = shifted(own.astype(bf16), "col", -1)
    diag = [shifted(piece, "col", -1) for piece in below]
    own_sum, right_sum, edges, below_sum, diag_sum = run_slots(
        counts, offset_y, offset_x, scale, obj_re, obj_im, right, below, diag, probe_re, probe_im, amplitude, out_parts
    )

    diag_in = [shifted(piece, "col", 1) for piece in diag_sum]
    right_in = shifted(right_sum, "col", 1)
    beside_right = shifted(edges[:, 0], "col", -1) + edges[:, 2]
    beside_left = shifted(edges[:, 1], "col", 1) + shifted(edges[:, 3], "col", 2)
    lower = [mine + theirs.astype(f32) for mine, theirs in zip(below_sum, diag_in)]
    below_in = [shifted(piece.astype(bf16), "row", 1) for piece in lower]

    def with_ends(row, at):
        chunks = row.reshape(2, side // LANES, LANES)
        ends = [jnp.broadcast_to(column[:, at, None, None], (2, 1, LANES)) for column in (beside_left, beside_right)]
        return jnp.concatenate([ends[0], chunks, ends[1]], axis=1)

    first = with_ends(own_sum[:, 0] + right_in[:, 0].astype(f32), 0)
    last = with_ends(own_sum[:, -1] + right_in[:, -1].astype(f32), side - 1)
    low_first = with_ends(lower[0][:, 0], side)
    low_last = with_ends(lower[-1][:, -1], 2 * side - 1)
    sides = jnp.concatenate([beside_left[:, side:], beside_right[:, side:]], axis=1)
    sent_down = jnp.concatenate([last, sides.reshape(2, -1, LANES)], axis=1)
    from_up = shifted(sent_down, "row", 1)
    from_down = shifted(first, "row", -1)
    from_far = shifted(low_last, "row", 2)
    rows = side // LANES + 2
    top = from_up[:, :rows] + from_far
    bottom = from_down + low_first
    spilled = from_up[:, rows:].reshape(2, 2, side)
    ring = jnp.concatenate([beside_left[:, :side] + spilled[:, 0], beside_right[:, :side] + spilled[:, 1]], axis=0)
    ring = jnp.concatenate([ring, jnp.zeros((4, side), f32)], axis=0)
    return run_finish(own_sum, right_in, below_in, top, bottom, ring)


def solution(mesh):
    split = P("row", "col")
    return jax.shard_map(
        body,
        mesh=mesh,
        in_specs=(split, split, P(), P(), P("row", "col", None, None), split, split, split),
        out_specs=(split, split),
        check_vma=False,
    )
```

```python
import functools
import math

import jax
import jax.numpy as jnp
import numpy as np
from jax import lax
from jax.experimental import pallas as pl
from jax.experimental.pallas import tpu as pltpu
from jax.sharding import PartitionSpec as P


modulus_floor = 0.5
shrink_level = 0.2
step_size = 0.5
epsilon = 1e-05
LANES = 128


def transform_tables(side):
    quarter, half = side // 4, side // 2
    bf16 = jnp.bfloat16

    def cos_sin(rows, cols):
        angle = (rows[:, None] * cols[None, :] % side) * (2.0 * math.pi / side)
        norm = 1.0 / math.sqrt(side)
        return np.cos(angle) * norm, -np.sin(angle) * norm

    base = np.arange(quarter)
    grouped = np.concatenate([base[c::4] for c in range(4)])
    rows_in, rows_out = [], []
    for c in range(4):
        members = 4 * base + c
        co, si = cos_sin(grouped, members)
        rows_in.append(np.block([[co, -si], [si, co]]))
        co, si = cos_sin(base, members)
        rows_out.append(np.block([[co, si], [-si, co]]))
    frequency = np.concatenate([np.arange(0, half, 2), np.arange(1, half, 2)])
    mirrored = (side - frequency) % side
    mirrored[0] = half
    every = np.arange(side)
    co, si = cos_sin(every, frequency)
    co[:, 0] = np.where(every % 2 == 0, co[:, 0], 0.0)
    si[:, 0] = np.where(every % 2 == 1, 1.0 / math.sqrt(side), 0.0)
    cols_in = np.concatenate([co, si], axis=1)
    cols_out = []
    for part in range(2):
        run = slice(part * quarter, (part + 1) * quarter)
        members = np.concatenate([frequency[run], mirrored[run]])
        co, si = cos_sin(members, np.arange(half))
        cols_out.append(np.block([[co, -si], [si, co]]))
    order = np.concatenate([frequency, mirrored])
    pick = np.zeros((side, side))
    pick[order, every] = 1.0
    return tuple(
        np.asarray(np.asarray(table, np.float32), dtype=bf16)
        for table in (np.stack(rows_in), cols_in, np.stack(cols_out), np.stack(rows_out), pick)
    )


def dot(left_op, right_op):
    return jnp.dot(left_op, right_op, preferred_element_type=jnp.float32)


def slots_kernel(side, in_parts, out_parts, *refs):
    refs = list(refs)

    def take(count):
        taken = refs[:count]
        del refs[:count]
        return taken

    count_ref, oy_ref, ox_ref, scale_ref, own_re, own_im, right_ref = take(7)
    below_refs, diag_refs = take(len(in_parts)), take(len(in_parts))
    probe_re, probe_im, amp_ref = take(3)
    rows_in, cols_in, cols_out, rows_out, pick = take(5)
    own_out, right_out, edge_out = take(3)
    below_outs, diag_outs = take(len(out_parts)), take(len(out_parts))
    region, sums, probe, exits, wide, half, delta, back, amp = refs
    quarter, chunks = side // 4, side // LANES
    f32, bf16 = jnp.float32, jnp.bfloat16

    for p in range(2):
        for a in range(chunks):
            lanes = slice(a * LANES, (a + 1) * LANES)
            own = (own_re, own_im)[p]
            region[p, a, :side, :] = own[:, lanes].astype(bf16).astype(f32)
            region[p, chunks + a, :side, :] = right_ref[p, :, lanes].astype(f32)
            at = side
            for rows, below_ref, diag_ref in zip(in_parts, below_refs, diag_refs):
                region[p, a, at : at + rows, :] = below_ref[p, :, lanes].astype(f32)
                region[p, chunks + a, at : at + rows, :] = diag_ref[p, :, lanes].astype(f32)
                at += rows
            probe[p, a] = (probe_re, probe_im)[p][:, lanes]
    sums[...] = jnp.zeros_like(sums)

    lane = lax.broadcasted_iota(jnp.int32, (1, LANES), 1)

    def one_slot(s, carry):
        oy = oy_ref[0, s]
        ox = ox_ref[0, s]
        q = ox // LANES
        b = ox % LANES
        inward = (LANES - b) % LANES
        keep = lane < LANES - b
        placed = lane >= b

        for c in range(4):
            rows = pl.ds(oy + c, quarter, stride=4)
            before = None
            for a in range(chunks + 1):
                now = [pltpu.roll(region[p, q + a, rows, :], inward, axis=1) for p in range(2)]
                if a > 0:
                    o_re, o_im = (jnp.where(keep, before[p], now[p]) for p in range(2))
                    mine = pl.ds(c, quarter, stride=4)
                    p_re, p_im = probe[0, a - 1, mine, :], probe[1, a - 1, mine, :]
                    lanes = slice((a - 1) * LANES, a * LANES)
                    exits[c, :quarter, lanes] = (p_re * o_re - p_im * o_im).astype(bf16)
                    exits[c, quarter:, lanes] = (p_re * o_im + p_im * o_re).astype(bf16)
                before = now
        for c in range(4):
            wide[c] = dot(rows_in[c], exits[c])
        step = quarter // 4
        for cc in range(4):
            for a in range(chunks):
                lanes = slice(a * LANES, (a + 1) * LANES)
                re = [wide[c, cc * step : (cc + 1) * step, lanes] for c in range(4)]
                im = [wide[c, quarter + cc * step : quarter + (cc + 1) * step, lanes] for c in range(4)]
                er, ei, fr, fi = re[0] + re[2], im[0] + im[2], re[0] - re[2], im[0] - im[2]
                gr, gi, hr, hi = re[1] + re[3], im[1] + im[3], re[1] - re[3], im[1] - im[3]
                outs = (
                    (er + gr, ei + gi),
                    (fr + hi, fi - hr),
                    (er - gr, ei - gi),
                    (fr - hi, fi + hr),
                )
                for m, (o_re, o_im) in enumerate(outs):
                    half[cc, m * step : (m + 1) * step, lanes] = o_re.astype(bf16)
                    half[cc, quarter + m * step : quarter + (m + 1) * step, lanes] = o_im.astype(bf16)

        ordered = dot(amp_ref[0, s], pick[...])
        for a in range(chunks):
            amp[a] = ordered[:, a * LANES : (a + 1) * LANES]

        for cc in range(4):
            wide[cc] = dot(half[cc], cols_in[...])
        mid = chunks // 2
        for cc in range(4):
            for part in range(mid):
                lo = slice(part * LANES, (part + 1) * LANES)
                hi = slice((mid + part) * LANES, (mid + part + 1) * LANES)
                p1, p3 = wide[cc, :quarter, lo], wide[cc, :quarter, hi]
                p4, p2 = wide[cc, quarter:, lo], wide[cc, quarter:, hi]
                if part == 0:
                    p2, p3 = jnp.where(lane == 0, -p3, p2), jnp.where(lane == 0, p2, p3)
                for sign in range(2):
                    s_re = p1 - p2 if sign == 0 else p1 + p2
                    s_im = p4 + p3 if sign == 0 else p4 - p3
                    measured = amp[sign * mid + part, pl.ds(cc, quarter, stride=4), :]
                    inverse = jnp.minimum(lax.rsqrt(s_re * s_re + s_im * s_im), 1.0 / modulus_floor)
                    factor = measured * inverse - 1.0
                    rows = slice(cc * quarter, (cc + 1) * quarter)
                    for k, value in ((sign, s_re), (2 + sign, s_im)):
                        delta[part, rows, k * LANES : (k + 1) * LANES] = (value * factor).astype(bf16)

        for part in range(2):
            for r in range(2):
                wide[2 * part + r] = dot(delta[part, r * side // 2 : (r + 1) * side // 2, :], cols_out[part])
        for cc in range(4):
            for k in range(2):
                for a in range(mid):
                    lanes = slice((k * mid + a) * LANES, (k * mid + a + 1) * LANES)
                    rows = slice((cc % 2) * quarter, (cc % 2 + 1) * quarter)
                    even, odd = wide[cc // 2, rows, lanes], wide[2 + cc // 2, rows, lanes]
                    put = slice(k * quarter, (k + 1) * quarter)
                    back[cc, put, a * LANES : (a + 1) * LANES] = (even + odd).astype(bf16)
                    back[cc, put, (mid + a) * LANES : (mid + a + 1) * LANES] = (even - odd).astype(bf16)

        for c in range(4):
            wide[c] = dot(rows_out[c], back[c])
        rows_at = 16
        for r in range(quarter // rows_at):
            before = [None] * 8
            for a in range(chunks + 1):
                now = [None] * 8
                if a < chunks:
                    lanes = slice(a * LANES, (a + 1) * LANES)
                    at = r * rows_at
                    re = [wide[c, at : at + rows_at, lanes] for c in range(4)]
                    im = [wide[c, quarter + at : quarter + at + rows_at, lanes] for c in range(4)]
                    er, ei, fr, fi = re[0] + re[2], im[0] + im[2], re[0] - re[2], im[0] - im[2]
                    gr, gi, hr, hi = re[1] + re[3], im[1] + im[3], re[1] - re[3], im[1] - im[3]
                    outs = (
                        (er + gr, ei + gi),
                        (fr - hi, fi + hr),
                        (er - gr, ei - gi),
                        (fr + hi, fi - hr),
                    )
                    for m, (w_re, w_im) in enumerate(outs):
                        mine = slice(m * quarter + at, m * quarter + at + rows_at)
                        p_re, p_im = probe[0, a, mine, :], probe[1, a, mine, :]
                        now[2 * m] = pltpu.roll(p_re * w_re + p_im * w_im, b, axis=1)
                        now[2 * m + 1] = pltpu.roll(p_re * w_im - p_im * w_re, b, axis=1)
                for k in range(8):
                    one = jnp.zeros((rows_at, LANES), f32) if now[k] is None else now[k]
                    two = jnp.zeros((rows_at, LANES), f32) if before[k] is None else before[k]
                    rows = pl.ds(oy + (k // 2) * quarter + r * rows_at, rows_at)
                    sums[k % 2, q + a, rows, :] += jnp.where(placed, one, two)
                before = now
        return carry

    lax.fori_loop(0, count_ref[0, 0], one_slot, 0)

    scale = scale_ref[0, 0]
    for p in range(2):
        own = (own_re, own_im)[p]
        for a in range(chunks):
            lanes = slice(a * LANES, (a + 1) * LANES)
            right_out[p, :, lanes] = (scale * sums[p, chunks + a, :side, :]).astype(bf16)
            own_out[p, :, lanes] = own[:, lanes] + scale * sums[p, a, :side, :]
            at = side
            for rows, below_out, diag_out in zip(out_parts, below_outs, diag_outs):
                below_out[p, :, lanes] = scale * sums[p, a, at : at + rows, :]
                diag_out[p, :, lanes] = (scale * sums[p, chunks + a, at : at + rows, :]).astype(bf16)
                at += rows
        for k, (a, at) in enumerate(((0, 0), (chunks - 1, LANES - 1), (chunks, 0), (2 * chunks - 1, LANES - 1))):
            for r in range(2 * side // LANES):
                cells = scale * sums[p, a, r * LANES : (r + 1) * LANES, :]
                if k < 2 and r < chunks:
                    cells += own[r * LANES : (r + 1) * LANES, a * LANES : (a + 1) * LANES]
                edge_out[k, p : p + 1, r * LANES : (r + 1) * LANES] = cells.T[at : at + 1, :]


def run_slots(counts, offset_y, offset_x, scale, obj_re, obj_im, right, below, diag, probe_re, probe_im, amplitude, out_parts):
    side = probe_re.shape[0]
    chunks, quarter = side // LANES, side // 4
    f32, bf16 = jnp.float32, jnp.bfloat16
    tables = transform_tables(side)
    in_parts = [part.shape[1] for part in below]
    smem = pl.BlockSpec(memory_space=pltpu.SMEM)
    vmem = pl.BlockSpec(memory_space=pltpu.VMEM)
    tile = lambda rows, kind: jax.ShapeDtypeStruct((2, rows, side), kind)
    outs = [tile(side, f32), tile(side, bf16), jax.ShapeDtypeStruct((4, 2, 2 * side), f32)]
    outs += [tile(rows, f32) for rows in out_parts] + [tile(rows, bf16) for rows in out_parts]
    results = pl.pallas_call(
        functools.partial(slots_kernel, side, in_parts, out_parts),
        out_shape=outs,
        in_specs=[smem] * 4 + [vmem] * (11 + 2 * len(in_parts)),
        out_specs=[vmem] * len(outs),
        scratch_shapes=[
            pltpu.VMEM((2, 2 * chunks, 2 * side, LANES), f32),
            pltpu.VMEM((2, 2 * chunks, 2 * side, LANES), f32),
            pltpu.VMEM((2, chunks, side, LANES), f32),
            pltpu.VMEM((4, 2 * quarter, side), bf16),
            pltpu.VMEM((4, 2 * quarter, side), f32),
            pltpu.VMEM((4, 2 * quarter, side), bf16),
            pltpu.VMEM((2, side, side), bf16),
            pltpu.VMEM((4, 2 * quarter, side), bf16),
            pltpu.VMEM((chunks, side, LANES), f32),
        ],
        compiler_params=pltpu.CompilerParams(vmem_limit_bytes=40 * 2**20),
        name="slots",
    )(counts, offset_y, offset_x, scale, obj_re, obj_im, right, *below, *diag, probe_re, probe_im, amplitude, *tables)
    parts = len(out_parts)
    return results[0], results[1], results[2], results[3 : 3 + parts], results[3 + parts :]


def finish_kernel(parts, *refs):
    own_ref, right_ref = refs[:2]
    below_refs = refs[2 : 2 + len(parts)]
    up_ref, far_ref, down_ref, low_ref, left_ref, beside_ref, out_re, out_im, cells, spill, result, ring_ref = refs[
        2 + len(parts) :
    ]
    side = own_ref.shape[1]
    chunks = side // LANES
    f32 = jnp.float32
    pad, count = 16, 8
    rows = chunks + 2
    for p in range(2):
        for k, column in enumerate((left_ref, beside_ref)):
            for a in range(chunks):
                lanes = slice(a * LANES, (a + 1) * LANES)
                at = rows + k * chunks + a
                ring_ref[2 * k + p : 2 * k + p + 1, lanes] = column[p : p + 1, lanes] + up_ref[p, at : at + 1, :]
    ring = ring_ref[...].T
    for p in range(2):
        for a in range(chunks):
            lanes = slice(a * LANES, (a + 1) * LANES)
            at = 0
            for rows, below_ref in zip(parts, below_refs):
                mine = slice(at, at + rows)
                cells[p, a + 1, pad + at : pad + at + rows, :] = (
                    own_ref[p, mine, lanes] + right_ref[p, mine, lanes].astype(f32) + below_ref[p, :, lanes].astype(f32)
                )
                at += rows
        for k in range(2):
            beside = jnp.broadcast_to(ring[:, 2 * k + p : 2 * k + p + 1], (side, LANES))
            cells[p, k * (chunks + 1), pad : pad + side, :] = beside
        for a in range(chunks + 2):
            one = slice(a, a + 1)
            cells[p, a, pad - 1 : pad, :] = up_ref[p, one, :] + far_ref[p, one, :]
            cells[p, a, pad + side : pad + side + 1, :] = down_ref[p, one, :] + low_ref[p, one, :]

    bound = 2.0 * shrink_level
    lane = lax.broadcasted_iota(jnp.int32, (count, LANES), 1)
    even, first, last = lane % 2 == 0, lane == 0, lane == LANES - 1
    cut = lambda t: jnp.clip(t, -bound, bound)
    later = lambda t: pltpu.roll(t, 1, axis=1)
    sooner = lambda t: pltpu.roll(t, LANES - 1, axis=1)

    def clips(total, gap, total_x, gap_x):
        side_by_side = cut(total - total_x)
        other = cut(gap + gap_x) + cut(gap - gap_x)
        return side_by_side + other, side_by_side - other

    def moved(p, at):
        upper = pl.ds(pad + 1 + 2 * at, count, stride=2)
        lower = pl.ds(pad + 2 + 2 * at, count, stride=2)
        high = [cells[p, a, upper, :] for a in range(chunks + 2)]
        low = [cells[p, a, lower, :] for a in range(chunks + 2)]
        fields = [[h + w for h, w in zip(high, low)], [h - w for h, w in zip(high, low)]]
        turned = []
        for field in fields:
            right_of = [later(field[a]) for a in range(chunks + 1)]
            left_of = [sooner(field[a]) for a in range(1, chunks + 2)]
            turned.append(
                [
                    jnp.where(
                        even,
                        jnp.where(first, right_of[a - 1], right_of[a]),
                        jnp.where(last, left_of[a], left_of[a - 1]),
                    )
                    for a in range(1, chunks + 1)
                ]
            )
        return [clips(fields[0][a + 1], fields[1][a + 1], turned[0][a], turned[1][a]) for a in range(chunks)]

    for p in range(2):
        for a, (_, below_one) in enumerate(moved(p, -count)):
            spill[p, a, 1 : 1 + count, :] = below_one

    def block(i, carry):
        at = pl.multiple_of(i * count, count)
        for p in range(2):
            shifted_clips = moved(p, at)
            for a in range(chunks):
                upper = pl.ds(pad + 2 * at, count, stride=2)
                lower = pl.ds(pad + 1 + 2 * at, count, stride=2)
                high, low = cells[p, a + 1, upper, :], cells[p, a + 1, lower, :]
                total, gap = high + low, high - low
                total_x = jnp.where(even, sooner(total), later(total))
                gap_x = jnp.where(even, sooner(gap), later(gap))
                top_clip, low_clip = clips(total, gap, total_x, gap_x)
                spill[p, a, pl.ds(at + count + 1, count), :] = shifted_clips[a][1]
                top_clip += spill[p, a, pl.ds(at + count, count), :]
                low_clip += shifted_clips[a][0]
                result[p, a, pl.ds(2 * at, count, stride=2), :] = high - 0.125 * top_clip
                result[p, a, pl.ds(2 * at + 1, count, stride=2), :] = low - 0.125 * low_clip
            for a in range(chunks):
                mine = pl.ds(2 * at, 2 * count)
                (out_re, out_im)[p][mine, a * LANES : (a + 1) * LANES] = result[p, a, mine, :]
        return carry

    lax.fori_loop(0, side // (2 * count), block, 0)


def run_finish(own, right, below, *edges):
    side = own.shape[1]
    chunks = side // LANES
    f32 = jnp.float32
    vmem = pl.BlockSpec(memory_space=pltpu.VMEM)
    tile = jax.ShapeDtypeStruct((side, side), f32)
    parts = [part.shape[1] for part in below]
    return pl.pallas_call(
        functools.partial(finish_kernel, parts),
        out_shape=(tile, tile),
        in_specs=[vmem] * (2 + len(parts) + len(edges)),
        out_specs=[vmem] * 2,
        scratch_shapes=[
            pltpu.VMEM((2, chunks + 2, side + 32, LANES), f32),
            pltpu.VMEM((2, chunks, side // 2 + 16, LANES), f32),
            pltpu.VMEM((2, chunks, side, LANES), f32),
            pltpu.VMEM((8, side), f32),
        ],
        compiler_params=pltpu.CompilerParams(vmem_limit_bytes=20 * 2**20),
        name="finish",
    )(own, right, *below, *edges)


def shifted(value, axis, steps):
    count = lax.axis_size(axis)
    return lax.ppermute(value, axis, [(i, (i + steps) % count) for i in range(count)])


def parts_of(side, weights):
    unit = side // 32
    sizes = [unit * weight for weight in weights]
    assert sum(sizes) == side and unit % 16 == 0
    return sizes


def split_rows(value, sizes):
    ends = np.cumsum(sizes)
    return [value[:, end - size : end] for end, size in zip(ends, sizes)]


def update(obj_re, obj_im, probe_re, probe_im, amplitude, offset_y, offset_x, counts):
    f32, bf16 = jnp.float32, jnp.bfloat16
    side = probe_re.shape[0]
    in_parts, out_parts = parts_of(side, IN_SHARES), parts_of(side, OUT_SHARES)

    head = in_parts[0]
    piece = jnp.stack([obj_re[:head], obj_im[:head]]).astype(bf16)
    piece, later_re, later_im = lax.optimization_barrier((piece, obj_re, obj_im))
    below = [shifted(piece, "row", -1)]
    own = jnp.stack([later_re, later_im]).astype(bf16)
    right = shifted(own, "col", -1)
    for rest in split_rows(own, in_parts)[1:]:
        below.append(shifted(rest, "row", -1))
    diag = [shifted(value, "col", -1) for value in below]
    probe_power = jnp.mean(probe_re * probe_re + probe_im * probe_im) + epsilon
    scale = (step_size / probe_power).reshape(1, 1)
    own_sum, right_sum, edges, below_sum, diag_sum = run_slots(
        counts, offset_y, offset_x, scale, obj_re, obj_im, right, below, diag, probe_re, probe_im, amplitude, out_parts
    )

    diag_in = [shifted(value, "col", 1) for value in diag_sum]
    beside_right = shifted(edges[0], "col", -1) + edges[2]
    beside_left = shifted(edges[1], "col", 1) + shifted(edges[3], "col", 2)
    right_in = shifted(right_sum, "col", 1)
    lower = [mine + theirs.astype(f32) for mine, theirs in zip(below_sum, diag_in)]
    below_in = [shifted(value.astype(bf16), "row", 1) for value in lower]

    def with_ends(row, at):
        chunks = row.reshape(2, side // LANES, LANES)
        ends = [jnp.broadcast_to(column[:, at, None, None], (2, 1, LANES)) for column in (beside_left, beside_right)]
        return jnp.concatenate([ends[0], chunks, ends[1]], axis=1)

    low_first = with_ends(lower[0][:, 0], side)
    low_last = with_ends(lower[-1][:, -1], 2 * side - 1)
    from_far = shifted(low_last, "row", 2)
    first = with_ends(own_sum[:, 0] + right_in[:, 0].astype(f32), 0)
    last = with_ends(own_sum[:, -1] + right_in[:, -1].astype(f32), side - 1)
    sides = jnp.concatenate([beside_left[:, side:], beside_right[:, side:]], axis=1)
    sent_down = jnp.concatenate([last, sides.reshape(2, -1, LANES)], axis=1)
    from_up = shifted(sent_down, "row", 1)
    from_down = shifted(first, "row", -1)
    return run_finish(own_sum, right_in, below_in, from_up, from_far, from_down, low_first, beside_left, beside_right)


IN_SHARES = (16, 10, 6)
OUT_SHARES = (4, 12, 16)


def solution(mesh):
    split = P("row", "col")
    return jax.shard_map(
        update,
        mesh=mesh,
        in_specs=(split, split, P(), P(), P("row", "col", None, None), split, split, split),
        out_specs=(split, split),
        check_vma=False,
    )
```

```python
import functools
import math

import jax
import jax.numpy as jnp
import numpy as np
from jax import lax
from jax.experimental import pallas as pl
from jax.experimental.pallas import tpu as pltpu
from jax.sharding import PartitionSpec as P


modulus_floor = 0.5
shrink_level = 0.2
step_size = 0.5
epsilon = 1e-05
LANES = 128


def transform_tables(side):
    quarter, half = side // 4, side // 2
    bf16 = jnp.bfloat16

    def cos_sin(rows, cols):
        angle = (rows[:, None] * cols[None, :] % side) * (2.0 * math.pi / side)
        norm = 1.0 / math.sqrt(side)
        return np.cos(angle) * norm, -np.sin(angle) * norm

    base = np.arange(quarter)
    grouped = np.concatenate([base[c::4] for c in range(4)])
    rows_in, rows_out = [], []
    for c in range(4):
        members = 4 * base + c
        co, si = cos_sin(grouped, members)
        rows_in.append(np.block([[co, -si], [si, co]]))
        co, si = cos_sin(base, members)
        rows_out.append(np.block([[co, si], [-si, co]]))
    frequency = np.concatenate([np.arange(0, half, 2), np.arange(1, half, 2)])
    mirrored = (side - frequency) % side
    mirrored[0] = half
    every = np.arange(side)
    co, si = cos_sin(every, frequency)
    co[:, 0] = np.where(every % 2 == 0, co[:, 0], 0.0)
    si[:, 0] = np.where(every % 2 == 1, 1.0 / math.sqrt(side), 0.0)
    cols_in = np.concatenate([co, si], axis=1)
    cols_out = []
    for part in range(2):
        run = slice(part * quarter, (part + 1) * quarter)
        members = np.concatenate([frequency[run], mirrored[run]])
        co, si = cos_sin(members, np.arange(half))
        cols_out.append(np.block([[co, -si], [si, co]]))
    order = np.concatenate([frequency, mirrored])
    pick = np.zeros((side, side))
    pick[order, every] = 1.0
    return tuple(
        np.asarray(np.asarray(table, np.float32), dtype=bf16)
        for table in (np.stack(rows_in), cols_in, np.stack(cols_out), np.stack(rows_out), pick)
    )


def dot(left_op, right_op):
    return jnp.dot(left_op, right_op, preferred_element_type=jnp.float32)


def slots_kernel(side, in_parts, out_parts, *refs):
    refs = list(refs)

    def take(count):
        taken = refs[:count]
        del refs[:count]
        return taken

    count_ref, oy_ref, ox_ref, scale_ref, own_re, own_im, right_ref = take(7)
    below_refs, diag_refs = take(len(in_parts)), take(len(in_parts))
    probe_re, probe_im, amp_ref = take(3)
    rows_in, cols_in, cols_out, rows_out, pick = take(5)
    own_out, right_out, edge_out = take(3)
    below_outs, diag_outs = take(len(out_parts)), take(len(out_parts))
    region, sums, probe, exits, wide, half, delta, back, amp, held, amp_held = refs[:11]
    table_held, sems, amp_sems, table_sems = refs[11:16], refs[16], refs[17], refs[18]
    quarter, chunks = side // 4, side // LANES
    f32, bf16 = jnp.float32, jnp.bfloat16

    def fetches(sources, target, at):
        return [
            pltpu.make_async_copy(
                sources[p].at[:, a * LANES : (a + 1) * LANES], target.at[p, a], sems.at[at + p * chunks + a]
            )
            for p in range(2)
            for a in range(chunks)
        ]

    def amp_fetch(s):
        return pltpu.make_async_copy(amp_ref.at[0, s], amp_held.at[s], amp_sems.at[s])

    own_copies = fetches((own_re, own_im), held, 0)
    late_copies = fetches((probe_re, probe_im), probe, 2 * chunks)
    tables = (rows_in, pick, cols_in, cols_out, rows_out)
    late_copies += [
        pltpu.make_async_copy(table, target, table_sems.at[k]) for k, (table, target) in enumerate(zip(tables, table_held))
    ]
    for copy in own_copies + late_copies:
        copy.start()

    def start_amp(s, carry):
        amp_fetch(s).start()
        return carry

    lax.fori_loop(0, count_ref[0, 0], start_amp, 0)
    rows_in, pick, cols_in, cols_out, rows_out = table_held
    sums[...] = jnp.zeros_like(sums)

    for p in range(2):
        for a in range(chunks):
            lanes = slice(a * LANES, (a + 1) * LANES)
            region[p, chunks + a, :side, :] = right_ref[p, :, lanes].astype(f32)
            at = side
            for rows, below_ref, diag_ref in zip(in_parts, below_refs, diag_refs):
                region[p, a, at : at + rows, :] = below_ref[p, :, lanes].astype(f32)
                region[p, chunks + a, at : at + rows, :] = diag_ref[p, :, lanes].astype(f32)
                at += rows
    for copy in own_copies:
        copy.wait()
    for p in range(2):
        for a in range(chunks):
            region[p, a, :side, :] = held[p, a].astype(bf16).astype(f32)
    for copy in late_copies:
        copy.wait()

    lane = lax.broadcasted_iota(jnp.int32, (1, LANES), 1)

    def one_slot(s, carry):
        oy = oy_ref[0, s]
        ox = ox_ref[0, s]
        q = ox // LANES
        b = ox % LANES
        inward = (LANES - b) % LANES
        keep = lane < LANES - b
        placed = lane >= b

        amp_fetch(s).wait()

        for c in range(4):
            rows = pl.ds(oy + c, quarter, stride=4)
            before = None
            for a in range(chunks + 1):
                now = [pltpu.roll(region[p, q + a, rows, :], inward, axis=1) for p in range(2)]
                if a > 0:
                    o_re, o_im = (jnp.where(keep, before[p], now[p]) for p in range(2))
                    mine = pl.ds(c, quarter, stride=4)
                    p_re, p_im = probe[0, a - 1, mine, :], probe[1, a - 1, mine, :]
                    lanes = slice((a - 1) * LANES, a * LANES)
                    exits[c, :quarter, lanes] = (p_re * o_re - p_im * o_im).astype(bf16)
                    exits[c, quarter:, lanes] = (p_re * o_im + p_im * o_re).astype(bf16)
                before = now
        for c in range(4):
            wide[c] = dot(rows_in[c], exits[c])
        step = quarter // 4
        for cc in range(4):
            for a in range(chunks):
                lanes = slice(a * LANES, (a + 1) * LANES)
                re = [wide[c, cc * step : (cc + 1) * step, lanes] for c in range(4)]
                im = [wide[c, quarter + cc * step : quarter + (cc + 1) * step, lanes] for c in range(4)]
                er, ei, fr, fi = re[0] + re[2], im[0] + im[2], re[0] - re[2], im[0] - im[2]
                gr, gi, hr, hi = re[1] + re[3], im[1] + im[3], re[1] - re[3], im[1] - im[3]
                outs = (
                    (er + gr, ei + gi),
                    (fr + hi, fi - hr),
                    (er - gr, ei - gi),
                    (fr - hi, fi + hr),
                )
                for m, (o_re, o_im) in enumerate(outs):
                    half[cc, m * step : (m + 1) * step, lanes] = o_re.astype(bf16)
                    half[cc, quarter + m * step : quarter + (m + 1) * step, lanes] = o_im.astype(bf16)

        ordered = dot(amp_held[s], pick[...])
        for a in range(chunks):
            amp[a] = ordered[:, a * LANES : (a + 1) * LANES]

        for cc in range(4):
            wide[cc] = dot(half[cc], cols_in[...])
        mid = chunks // 2
        for cc in range(4):
            for part in range(mid):
                lo = slice(part * LANES, (part + 1) * LANES)
                hi = slice((mid + part) * LANES, (mid + part + 1) * LANES)
                p1, p3 = wide[cc, :quarter, lo], wide[cc, :quarter, hi]
                p4, p2 = wide[cc, quarter:, lo], wide[cc, quarter:, hi]
                if part == 0:
                    p2, p3 = jnp.where(lane == 0, -p3, p2), jnp.where(lane == 0, p2, p3)
                for sign in range(2):
                    s_re = p1 - p2 if sign == 0 else p1 + p2
                    s_im = p4 + p3 if sign == 0 else p4 - p3
                    measured = amp[sign * mid + part, pl.ds(cc, quarter, stride=4), :]
                    inverse = jnp.minimum(lax.rsqrt(s_re * s_re + s_im * s_im), 1.0 / modulus_floor)
                    factor = measured * inverse - 1.0
                    rows = slice(cc * quarter, (cc + 1) * quarter)
                    for k, value in ((sign, s_re), (2 + sign, s_im)):
                        delta[part, rows, k * LANES : (k + 1) * LANES] = (value * factor).astype(bf16)

        for part in range(2):
            for r in range(2):
                wide[2 * part + r] = dot(delta[part, r * side // 2 : (r + 1) * side // 2, :], cols_out[part])
        for cc in range(4):
            for k in range(2):
                for a in range(mid):
                    lanes = slice((k * mid + a) * LANES, (k * mid + a + 1) * LANES)
                    rows = slice((cc % 2) * quarter, (cc % 2 + 1) * quarter)
                    even, odd = wide[cc // 2, rows, lanes], wide[2 + cc // 2, rows, lanes]
                    put = slice(k * quarter, (k + 1) * quarter)
                    back[cc, put, a * LANES : (a + 1) * LANES] = (even + odd).astype(bf16)
                    back[cc, put, (mid + a) * LANES : (mid + a + 1) * LANES] = (even - odd).astype(bf16)

        for c in range(4):
            wide[c] = dot(rows_out[c], back[c])
        rows_at = 16
        for r in range(quarter // rows_at):
            before = [None] * 8
            for a in range(chunks + 1):
                now = [None] * 8
                if a < chunks:
                    lanes = slice(a * LANES, (a + 1) * LANES)
                    at = r * rows_at
                    re = [wide[c, at : at + rows_at, lanes] for c in range(4)]
                    im = [wide[c, quarter + at : quarter + at + rows_at, lanes] for c in range(4)]
                    er, ei, fr, fi = re[0] + re[2], im[0] + im[2], re[0] - re[2], im[0] - im[2]
                    gr, gi, hr, hi = re[1] + re[3], im[1] + im[3], re[1] - re[3], im[1] - im[3]
                    outs = (
                        (er + gr, ei + gi),
                        (fr - hi, fi + hr),
                        (er - gr, ei - gi),
                        (fr + hi, fi - hr),
                    )
                    for m, (w_re, w_im) in enumerate(outs):
                        mine = slice(m * quarter + at, m * quarter + at + rows_at)
                        p_re, p_im = probe[0, a, mine, :], probe[1, a, mine, :]
                        now[2 * m] = pltpu.roll(p_re * w_re + p_im * w_im, b, axis=1)
                        now[2 * m + 1] = pltpu.roll(p_re * w_im - p_im * w_re, b, axis=1)
                for k in range(8):
                    one = jnp.zeros((rows_at, LANES), f32) if now[k] is None else now[k]
                    two = jnp.zeros((rows_at, LANES), f32) if before[k] is None else before[k]
                    rows = pl.ds(oy + (k // 2) * quarter + r * rows_at, rows_at)
                    sums[k % 2, q + a, rows, :] += jnp.where(placed, one, two)
                before = now
        return carry

    lax.fori_loop(0, count_ref[0, 0], one_slot, 0)

    scale = scale_ref[0, 0]
    for p in range(2):
        for a in range(chunks):
            lanes = slice(a * LANES, (a + 1) * LANES)
            right_out[p, :, lanes] = (scale * sums[p, chunks + a, :side, :]).astype(bf16)
            own_out[p, :, lanes] = held[p, a] + scale * sums[p, a, :side, :]
            at = side
            for rows, below_out, diag_out in zip(out_parts, below_outs, diag_outs):
                below_out[p, :, lanes] = scale * sums[p, a, at : at + rows, :]
                diag_out[p, :, lanes] = (scale * sums[p, chunks + a, at : at + rows, :]).astype(bf16)
                at += rows
        for k, (a, at) in enumerate(((0, 0), (chunks - 1, LANES - 1), (chunks, 0), (2 * chunks - 1, LANES - 1))):
            for r in range(2 * side // LANES):
                cells = scale * sums[p, a, r * LANES : (r + 1) * LANES, :]
                if k < 2 and r < chunks:
                    cells += held[p, a, r * LANES : (r + 1) * LANES, :]
                edge_out[k, p : p + 1, r * LANES : (r + 1) * LANES] = cells.T[at : at + 1, :]


def run_slots(counts, offset_y, offset_x, scale, obj_re, obj_im, right, below, diag, probe_re, probe_im, amplitude, out_parts):
    side = probe_re.shape[0]
    chunks, quarter = side // LANES, side // 4
    f32, bf16 = jnp.float32, jnp.bfloat16
    tables = transform_tables(side)
    in_parts = [part.shape[1] for part in below]
    smem = pl.BlockSpec(memory_space=pltpu.SMEM)
    vmem = pl.BlockSpec(memory_space=pltpu.VMEM)
    here = pl.BlockSpec(memory_space=pl.ANY)
    slots = amplitude.shape[1]
    tile = lambda rows, kind: jax.ShapeDtypeStruct((2, rows, side), kind)
    outs = [tile(side, f32), tile(side, bf16), jax.ShapeDtypeStruct((4, 2, 2 * side), f32)]
    outs += [tile(rows, f32) for rows in out_parts] + [tile(rows, bf16) for rows in out_parts]
    results = pl.pallas_call(
        functools.partial(slots_kernel, side, in_parts, out_parts),
        out_shape=outs,
        in_specs=[smem] * 4 + [here] * 2 + [vmem] * (1 + 2 * len(in_parts)) + [here] * 8,
        out_specs=[vmem] * len(outs),
        scratch_shapes=[
            pltpu.VMEM((2, 2 * chunks, 2 * side, LANES), f32),
            pltpu.VMEM((2, 2 * chunks, 2 * side, LANES), f32),
            pltpu.VMEM((2, chunks, side, LANES), f32),
            pltpu.VMEM((4, 2 * quarter, side), bf16),
            pltpu.VMEM((4, 2 * quarter, side), f32),
            pltpu.VMEM((4, 2 * quarter, side), bf16),
            pltpu.VMEM((2, side, side), bf16),
            pltpu.VMEM((4, 2 * quarter, side), bf16),
            pltpu.VMEM((chunks, side, LANES), f32),
            pltpu.VMEM((2, chunks, side, LANES), f32),
            pltpu.VMEM((slots, side, side), bf16),
            *[pltpu.VMEM(tables[k].shape, bf16) for k in (0, 4, 1, 2, 3)],
            pltpu.SemaphoreType.DMA((4 * chunks,)),
            pltpu.SemaphoreType.DMA((slots,)),
            pltpu.SemaphoreType.DMA((5,)),
        ],
        compiler_params=pltpu.CompilerParams(vmem_limit_bytes=44 * 2**20),
        name="slots",
    )(counts, offset_y, offset_x, scale, obj_re, obj_im, right, *below, *diag, probe_re, probe_im, amplitude, *tables)
    parts = len(out_parts)
    return results[0], results[1], results[2], results[3 : 3 + parts], results[3 + parts :]


def finish_kernel(parts, *refs):
    own_ref, right_ref = refs[:2]
    below_refs = refs[2 : 2 + len(parts)]
    up_ref, far_ref, down_ref, low_ref, left_ref, beside_ref, out_re, out_im, cells, spill, result, ring_ref = refs[
        2 + len(parts) :
    ]
    side = own_ref.shape[1]
    chunks = side // LANES
    f32 = jnp.float32
    pad, count = 16, 8
    rows = chunks + 2
    for p in range(2):
        for k, column in enumerate((left_ref, beside_ref)):
            for a in range(chunks):
                lanes = slice(a * LANES, (a + 1) * LANES)
                at = rows + k * chunks + a
                ring_ref[2 * k + p : 2 * k + p + 1, lanes] = column[p : p + 1, lanes] + up_ref[p, at : at + 1, :]
    ring = ring_ref[...].T
    for p in range(2):
        for a in range(chunks):
            lanes = slice(a * LANES, (a + 1) * LANES)
            at = 0
            for rows, below_ref in zip(parts, below_refs):
                mine = slice(at, at + rows)
                cells[p, a + 1, pad + at : pad + at + rows, :] = (
                    own_ref[p, mine, lanes] + right_ref[p, mine, lanes].astype(f32) + below_ref[p, :, lanes].astype(f32)
                )
                at += rows
        for k in range(2):
            beside = jnp.broadcast_to(ring[:, 2 * k + p : 2 * k + p + 1], (side, LANES))
            cells[p, k * (chunks + 1), pad : pad + side, :] = beside
        for a in range(chunks + 2):
            one = slice(a, a + 1)
            cells[p, a, pad - 1 : pad, :] = up_ref[p, one, :] + far_ref[p, one, :]
            cells[p, a, pad + side : pad + side + 1, :] = down_ref[p, one, :] + low_ref[p, one, :]

    bound = 2.0 * shrink_level
    lane = lax.broadcasted_iota(jnp.int32, (count, LANES), 1)
    even, first, last = lane % 2 == 0, lane == 0, lane == LANES - 1
    cut = lambda t: jnp.clip(t, -bound, bound)
    later = lambda t: pltpu.roll(t, 1, axis=1)
    sooner = lambda t: pltpu.roll(t, LANES - 1, axis=1)

    def clips(total, gap, total_x, gap_x):
        side_by_side = cut(total - total_x)
        other = cut(gap + gap_x) + cut(gap - gap_x)
        return side_by_side + other, side_by_side - other

    def moved(p, at):
        upper = pl.ds(pad + 1 + 2 * at, count, stride=2)
        lower = pl.ds(pad + 2 + 2 * at, count, stride=2)
        high = [cells[p, a, upper, :] for a in range(chunks + 2)]
        low = [cells[p, a, lower, :] for a in range(chunks + 2)]
        fields = [[h + w for h, w in zip(high, low)], [h - w for h, w in zip(high, low)]]
        turned = []
        for field in fields:
            right_of = [later(field[a]) for a in range(chunks + 1)]
            left_of = [sooner(field[a]) for a in range(1, chunks + 2)]
            turned.append(
                [
                    jnp.where(
                        even,
                        jnp.where(first, right_of[a - 1], right_of[a]),
                        jnp.where(last, left_of[a], left_of[a - 1]),
                    )
                    for a in range(1, chunks + 1)
                ]
            )
        return [clips(fields[0][a + 1], fields[1][a + 1], turned[0][a], turned[1][a]) for a in range(chunks)]

    for p in range(2):
        for a, (_, below_one) in enumerate(moved(p, -count)):
            spill[p, a, 1 : 1 + count, :] = below_one

    def block(i, carry):
        at = pl.multiple_of(i * count, count)
        for p in range(2):
            shifted_clips = moved(p, at)
            for a in range(chunks):
                upper = pl.ds(pad + 2 * at, count, stride=2)
                lower = pl.ds(pad + 1 + 2 * at, count, stride=2)
                high, low = cells[p, a + 1, upper, :], cells[p, a + 1, lower, :]
                total, gap = high + low, high - low
                total_x = jnp.where(even, sooner(total), later(total))
                gap_x = jnp.where(even, sooner(gap), later(gap))
                top_clip, low_clip = clips(total, gap, total_x, gap_x)
                spill[p, a, pl.ds(at + count + 1, count), :] = shifted_clips[a][1]
                top_clip += spill[p, a, pl.ds(at + count, count), :]
                low_clip += shifted_clips[a][0]
                result[p, a, pl.ds(2 * at, count, stride=2), :] = high - 0.125 * top_clip
                result[p, a, pl.ds(2 * at + 1, count, stride=2), :] = low - 0.125 * low_clip
            for a in range(chunks):
                mine = pl.ds(2 * at, 2 * count)
                (out_re, out_im)[p][mine, a * LANES : (a + 1) * LANES] = result[p, a, mine, :]
        return carry

    lax.fori_loop(0, side // (2 * count), block, 0)


def run_finish(own, right, below, *edges):
    side = own.shape[1]
    chunks = side // LANES
    f32 = jnp.float32
    vmem = pl.BlockSpec(memory_space=pltpu.VMEM)
    tile = jax.ShapeDtypeStruct((side, side), f32)
    parts = [part.shape[1] for part in below]
    return pl.pallas_call(
        functools.partial(finish_kernel, parts),
        out_shape=(tile, tile),
        in_specs=[vmem] * (2 + len(parts) + len(edges)),
        out_specs=[vmem] * 2,
        scratch_shapes=[
            pltpu.VMEM((2, chunks + 2, side + 32, LANES), f32),
            pltpu.VMEM((2, chunks, side // 2 + 16, LANES), f32),
            pltpu.VMEM((2, chunks, side, LANES), f32),
            pltpu.VMEM((8, side), f32),
        ],
        compiler_params=pltpu.CompilerParams(vmem_limit_bytes=20 * 2**20),
        name="finish",
    )(own, right, *below, *edges)


def shifted(value, axis, steps):
    count = lax.axis_size(axis)
    return lax.ppermute(value, axis, [(i, (i + steps) % count) for i in range(count)])


def parts_of(side, weights):
    unit = side // 32
    sizes = [unit * weight for weight in weights]
    assert sum(sizes) == side and unit % 16 == 0
    return sizes


def split_rows(value, sizes):
    ends = np.cumsum(sizes)
    return [value[:, end - size : end] for end, size in zip(ends, sizes)]


def update(obj_re, obj_im, probe_re, probe_im, amplitude, offset_y, offset_x, counts):
    f32, bf16 = jnp.float32, jnp.bfloat16
    side = probe_re.shape[0]
    in_parts, out_parts = parts_of(side, IN_SHARES), parts_of(side, OUT_SHARES)

    head = in_parts[0]
    piece = jnp.stack([obj_re[:head], obj_im[:head]]).astype(bf16)
    piece, later_re, later_im = lax.optimization_barrier((piece, obj_re, obj_im))
    below = [shifted(piece, "row", -1)]
    own = jnp.stack([later_re, later_im]).astype(bf16)
    right = shifted(own, "col", -1)
    for rest in split_rows(own, in_parts)[1:]:
        below.append(shifted(rest, "row", -1))
    diag = [shifted(value, "col", -1) for value in below]
    probe_power = jnp.mean(probe_re * probe_re + probe_im * probe_im) + epsilon
    scale = (step_size / probe_power).reshape(1, 1)
    own_sum, right_sum, edges, below_sum, diag_sum = run_slots(
        counts, offset_y, offset_x, scale, obj_re, obj_im, right, below, diag, probe_re, probe_im, amplitude, out_parts
    )

    diag_in = [shifted(value, "col", 1) for value in diag_sum]
    from_beside = shifted(edges[0], "col", -1)
    from_left, from_second = shifted(edges[1], "col", 1), shifted(edges[3], "col", 2)
    beside_right = from_beside + edges[2]
    beside_left = from_left + from_second
    right_in = shifted(right_sum, "col", 1)
    lower, below_in = [], []
    for mine, theirs in zip(below_sum, diag_in):
        lower.append(mine + theirs.astype(f32))
        sent = lower[-1].astype(bf16)
        below_in.append(shifted(sent, "row", 1))

    def with_ends(row, at):
        chunks = row.reshape(2, side // LANES, LANES)
        ends = [jnp.broadcast_to(column[:, at, None, None], (2, 1, LANES)) for column in (beside_left, beside_right)]
        return jnp.concatenate([ends[0], chunks, ends[1]], axis=1)

    low_first = with_ends(lower[0][:, 0], side)
    low_last = with_ends(lower[-1][:, -1], 2 * side - 1)
    from_far = shifted(low_last, "row", 2)
    first = with_ends(own_sum[:, 0] + right_in[:, 0].astype(f32), 0)
    last = with_ends(own_sum[:, -1] + right_in[:, -1].astype(f32), side - 1)
    sides = jnp.concatenate([beside_left[:, side:], beside_right[:, side:]], axis=1)
    sent_down = jnp.concatenate([last, sides.reshape(2, -1, LANES)], axis=1)
    from_up = shifted(sent_down, "row", 1)
    from_down = shifted(first, "row", -1)
    return run_finish(own_sum, right_in, below_in, from_up, from_far, from_down, low_first, beside_left, beside_right)


IN_SHARES = (16, 12, 4)
OUT_SHARES = (4, 12, 16)


def solution(mesh):
    split = P("row", "col")
    return jax.shard_map(
        update,
        mesh=mesh,
        in_specs=(split, split, P(), P(), P("row", "col", None, None), split, split, split),
        out_specs=(split, split),
        check_vma=False,
    )
```

```python
import functools
import math

import jax
import jax.numpy as jnp
import numpy as np
from jax import lax
from jax.experimental import pallas as pl
from jax.experimental.pallas import tpu as pltpu
from jax.sharding import PartitionSpec as P


modulus_floor = 0.5
shrink_level = 0.2
step_size = 0.5
epsilon = 1e-05
LANES = 128
UNROLL = 4


def transform_tables(side):
    quarter, half = side // 4, side // 2
    bf16 = jnp.bfloat16

    def cos_sin(rows, cols):
        angle = (rows[:, None] * cols[None, :] % side) * (2.0 * math.pi / side)
        norm = 1.0 / math.sqrt(side)
        return np.cos(angle) * norm, -np.sin(angle) * norm

    base = np.arange(quarter)
    grouped = np.concatenate([base[c::4] for c in range(4)])
    rows_in, rows_out = [], []
    for c in range(4):
        members = 4 * base + c
        co, si = cos_sin(grouped, members)
        rows_in.append(np.block([[co, -si], [si, co]]))
        co, si = cos_sin(base, members)
        rows_out.append(np.block([[co, si], [-si, co]]))
    frequency = np.concatenate([np.arange(0, half, 2), np.arange(1, half, 2)])
    mirrored = (side - frequency) % side
    mirrored[0] = half
    every = np.arange(side)
    co, si = cos_sin(every, frequency)
    co[:, 0] = np.where(every % 2 == 0, co[:, 0], 0.0)
    si[:, 0] = np.where(every % 2 == 1, 1.0 / math.sqrt(side), 0.0)
    cols_in = np.concatenate([co, si], axis=1)
    cols_out = []
    for part in range(2):
        run = slice(part * quarter, (part + 1) * quarter)
        members = np.concatenate([frequency[run], mirrored[run]])
        co, si = cos_sin(members, np.arange(half))
        cols_out.append(np.block([[co, -si], [si, co]]))
    order = np.concatenate([frequency, mirrored])
    pick = np.zeros((side, side))
    pick[order, every] = 1.0
    return tuple(
        np.asarray(np.asarray(table, np.float32), dtype=bf16)
        for table in (np.stack(rows_in), cols_in, np.stack(cols_out), np.stack(rows_out), pick)
    )


def dot(left_op, right_op):
    return jnp.dot(left_op, right_op, preferred_element_type=jnp.float32)


def slots_kernel(side, in_parts, out_parts, *refs):
    refs = list(refs)

    def take(count):
        taken = refs[:count]
        del refs[:count]
        return taken

    count_ref, oy_ref, ox_ref, scale_ref, own_re, own_im, right_ref = take(7)
    below_refs, diag_refs = take(len(in_parts)), take(len(in_parts))
    probe_re, probe_im, amp_ref = take(3)
    rows_in, cols_in, cols_out, rows_out, pick = take(5)
    own_out, right_out, left_out, beside_out, kept_out, second_out = take(6)
    below_outs, diag_outs = take(len(out_parts)), take(len(out_parts))
    region, sums, probe, exits, wide, half, delta, back, amp, held, amp_held = refs[:11]
    table_held, sems, amp_sems, table_sems = refs[11:16], refs[16], refs[17], refs[18]
    quarter, chunks = side // 4, side // LANES
    f32, bf16 = jnp.float32, jnp.bfloat16

    def fetches(sources, target, at):
        return [
            pltpu.make_async_copy(
                sources[p].at[:, a * LANES : (a + 1) * LANES], target.at[p, a], sems.at[at + p * chunks + a]
            )
            for p in range(2)
            for a in range(chunks)
        ]

    def amp_fetch(s):
        return pltpu.make_async_copy(amp_ref.at[0, s], amp_held.at[s], amp_sems.at[s])

    own_copies = fetches((own_re, own_im), held, 0)
    late_copies = fetches((probe_re, probe_im), probe, 2 * chunks)
    tables = (rows_in, pick, cols_in, cols_out, rows_out)
    late_copies += [
        pltpu.make_async_copy(table, target, table_sems.at[k]) for k, (table, target) in enumerate(zip(tables, table_held))
    ]
    for copy in own_copies + late_copies:
        copy.start()

    def start_amp(s, carry):
        amp_fetch(s).start()
        return carry

    lax.fori_loop(0, count_ref[0, 0], start_amp, 0)
    rows_in, pick, cols_in, cols_out, rows_out = table_held
    sums[...] = jnp.zeros_like(sums)

    for p in range(2):
        for a in range(chunks):
            lanes = slice(a * LANES, (a + 1) * LANES)
            region[p, chunks + a, :side, :] = right_ref[p, :, lanes].astype(f32)
            at = side
            for rows, below_ref, diag_ref in zip(in_parts, below_refs, diag_refs):
                region[p, a, at : at + rows, :] = below_ref[p, :, lanes].astype(f32)
                region[p, chunks + a, at : at + rows, :] = diag_ref[p, :, lanes].astype(f32)
                at += rows
    for copy in own_copies:
        copy.wait()
    for p in range(2):
        for a in range(chunks):
            region[p, a, :side, :] = held[p, a].astype(bf16).astype(f32)
    for copy in late_copies:
        copy.wait()

    lane = lax.broadcasted_iota(jnp.int32, (1, LANES), 1)

    def one_slot(s, carry):
        oy = oy_ref[0, s]
        ox = ox_ref[0, s]
        q = ox // LANES
        b = ox % LANES
        inward = (LANES - b) % LANES
        keep = lane < LANES - b
        placed = lane >= b

        amp_fetch(s).wait()

        for c in range(4):
            rows = pl.ds(oy + c, quarter, stride=4)
            before = None
            for a in range(chunks + 1):
                now = [pltpu.roll(region[p, q + a, rows, :], inward, axis=1) for p in range(2)]
                if a > 0:
                    o_re, o_im = (jnp.where(keep, before[p], now[p]) for p in range(2))
                    mine = pl.ds(c, quarter, stride=4)
                    p_re, p_im = probe[0, a - 1, mine, :], probe[1, a - 1, mine, :]
                    lanes = slice((a - 1) * LANES, a * LANES)
                    exits[c, :quarter, lanes] = (p_re * o_re - p_im * o_im).astype(bf16)
                    exits[c, quarter:, lanes] = (p_re * o_im + p_im * o_re).astype(bf16)
                before = now
        for c in range(4):
            wide[c] = dot(rows_in[c], exits[c])
        step = quarter // 4
        for cc in range(4):
            for a in range(chunks):
                lanes = slice(a * LANES, (a + 1) * LANES)
                re = [wide[c, cc * step : (cc + 1) * step, lanes] for c in range(4)]
                im = [wide[c, quarter + cc * step : quarter + (cc + 1) * step, lanes] for c in range(4)]
                er, ei, fr, fi = re[0] + re[2], im[0] + im[2], re[0] - re[2], im[0] - im[2]
                gr, gi, hr, hi = re[1] + re[3], im[1] + im[3], re[1] - re[3], im[1] - im[3]
                outs = (
                    (er + gr, ei + gi),
                    (fr + hi, fi - hr),
                    (er - gr, ei - gi),
                    (fr - hi, fi + hr),
                )
                for m, (o_re, o_im) in enumerate(outs):
                    half[cc, m * step : (m + 1) * step, lanes] = o_re.astype(bf16)
                    half[cc, quarter + m * step : quarter + (m + 1) * step, lanes] = o_im.astype(bf16)

        ordered = dot(amp_held[s], pick[...])
        for a in range(chunks):
            amp[a] = ordered[:, a * LANES : (a + 1) * LANES]

        for cc in range(4):
            wide[cc] = dot(half[cc], cols_in[...])
        mid = chunks // 2
        for cc in range(4):
            for part in range(mid):
                lo = slice(part * LANES, (part + 1) * LANES)
                hi = slice((mid + part) * LANES, (mid + part + 1) * LANES)
                p1, p3 = wide[cc, :quarter, lo], wide[cc, :quarter, hi]
                p4, p2 = wide[cc, quarter:, lo], wide[cc, quarter:, hi]
                if part == 0:
                    p2, p3 = jnp.where(lane == 0, -p3, p2), jnp.where(lane == 0, p2, p3)
                for sign in range(2):
                    s_re = p1 - p2 if sign == 0 else p1 + p2
                    s_im = p4 + p3 if sign == 0 else p4 - p3
                    measured = amp[sign * mid + part, pl.ds(cc, quarter, stride=4), :]
                    inverse = jnp.minimum(lax.rsqrt(s_re * s_re + s_im * s_im), 1.0 / modulus_floor)
                    factor = measured * inverse - 1.0
                    rows = slice(cc * quarter, (cc + 1) * quarter)
                    for k, value in ((sign, s_re), (2 + sign, s_im)):
                        delta[part, rows, k * LANES : (k + 1) * LANES] = (value * factor).astype(bf16)

        for part in range(2):
            for r in range(2):
                wide[2 * part + r] = dot(delta[part, r * side // 2 : (r + 1) * side // 2, :], cols_out[part])
        for cc in range(4):
            for k in range(2):
                for a in range(mid):
                    lanes = slice((k * mid + a) * LANES, (k * mid + a + 1) * LANES)
                    rows = slice((cc % 2) * quarter, (cc % 2 + 1) * quarter)
                    even, odd = wide[cc // 2, rows, lanes], wide[2 + cc // 2, rows, lanes]
                    put = slice(k * quarter, (k + 1) * quarter)
                    back[cc, put, a * LANES : (a + 1) * LANES] = (even + odd).astype(bf16)
                    back[cc, put, (mid + a) * LANES : (mid + a + 1) * LANES] = (even - odd).astype(bf16)

        for c in range(4):
            wide[c] = dot(rows_out[c], back[c])
        rows_at = 16
        for r in range(quarter // rows_at):
            before = [None] * 8
            for a in range(chunks + 1):
                now = [None] * 8
                if a < chunks:
                    lanes = slice(a * LANES, (a + 1) * LANES)
                    at = r * rows_at
                    re = [wide[c, at : at + rows_at, lanes] for c in range(4)]
                    im = [wide[c, quarter + at : quarter + at + rows_at, lanes] for c in range(4)]
                    er, ei, fr, fi = re[0] + re[2], im[0] + im[2], re[0] - re[2], im[0] - im[2]
                    gr, gi, hr, hi = re[1] + re[3], im[1] + im[3], re[1] - re[3], im[1] - im[3]
                    outs = (
                        (er + gr, ei + gi),
                        (fr - hi, fi + hr),
                        (er - gr, ei - gi),
                        (fr + hi, fi - hr),
                    )
                    for m, (w_re, w_im) in enumerate(outs):
                        mine = slice(m * quarter + at, m * quarter + at + rows_at)
                        p_re, p_im = probe[0, a, mine, :], probe[1, a, mine, :]
                        now[2 * m] = pltpu.roll(p_re * w_re + p_im * w_im, b, axis=1)
                        now[2 * m + 1] = pltpu.roll(p_re * w_im - p_im * w_re, b, axis=1)
                for k in range(8):
                    one = jnp.zeros((rows_at, LANES), f32) if now[k] is None else now[k]
                    two = jnp.zeros((rows_at, LANES), f32) if before[k] is None else before[k]
                    rows = pl.ds(oy + (k // 2) * quarter + r * rows_at, rows_at)
                    sums[k % 2, q + a, rows, :] += jnp.where(placed, one, two)
                before = now
        return carry

    lax.fori_loop(0, count_ref[0, 0], one_slot, 0)

    scale = scale_ref[0, 0]
    for p in range(2):
        for a in range(chunks):
            lanes = slice(a * LANES, (a + 1) * LANES)
            right_out[p, :, lanes] = (scale * sums[p, chunks + a, :side, :]).astype(bf16)
            own_out[p, :, lanes] = held[p, a] + scale * sums[p, a, :side, :]
            at = side
            for rows, below_out, diag_out in zip(out_parts, below_outs, diag_outs):
                below_out[p, :, lanes] = scale * sums[p, a, at : at + rows, :]
                diag_out[p, :, lanes] = (scale * sums[p, chunks + a, at : at + rows, :]).astype(bf16)
                at += rows
        here = slice(p, p + 1)
        columns = (
            (left_out, 0, 0, True),
            (beside_out, chunks - 1, LANES - 1, True),
            (kept_out, chunks, 0, False),
            (second_out, 2 * chunks - 1, LANES - 1, False),
        )
        for target, a, at, with_own in columns:
            cells = scale * sums[p, a]
            turned = jnp.concatenate([cells[r * LANES : (r + 1) * LANES, :].T[at : at + 1, :] for r in range(2 * chunks)], axis=1)
            if with_own:
                own_turned = [held[p, a, r * LANES : (r + 1) * LANES, :].T[at : at + 1, :] for r in range(chunks)]
                turned += jnp.concatenate(own_turned + [jnp.zeros((1, side), f32)], axis=1)
            target[here, : 2 * side] = turned
        for k, row in enumerate((0, side - 1, side, 2 * side - 1)):
            for a in range(chunks):
                at = 2 * side + k * side + a * LANES
                mine = scale * sums[p, a, row : row + 1, :]
                if k < 2:
                    mine += held[p, a, row : row + 1, :]
                kept_out[here, at : at + LANES] = mine
                beside_out[here, at : at + LANES] = scale * sums[p, chunks + a, row : row + 1, :]


def run_slots(counts, offset_y, offset_x, scale, obj_re, obj_im, right, below, diag, probe_re, probe_im, amplitude, out_parts):
    side = probe_re.shape[0]
    chunks, quarter = side // LANES, side // 4
    f32, bf16 = jnp.float32, jnp.bfloat16
    tables = transform_tables(side)
    in_parts = [part.shape[1] for part in below]
    smem = pl.BlockSpec(memory_space=pltpu.SMEM)
    vmem = pl.BlockSpec(memory_space=pltpu.VMEM)
    here = pl.BlockSpec(memory_space=pl.ANY)
    slots = amplitude.shape[1]
    tile = lambda rows, kind: jax.ShapeDtypeStruct((2, rows, side), kind)
    outs = [tile(side, f32), tile(side, bf16)] + [jax.ShapeDtypeStruct((2, n * side), f32) for n in (2, 6, 6, 2)]
    outs += [tile(rows, f32) for rows in out_parts] + [tile(rows, bf16) for rows in out_parts]
    results = pl.pallas_call(
        functools.partial(slots_kernel, side, in_parts, out_parts),
        out_shape=outs,
        in_specs=[smem] * 4 + [here] * 2 + [vmem] * (1 + 2 * len(in_parts)) + [here] * 8,
        out_specs=[vmem] * len(outs),
        scratch_shapes=[
            pltpu.VMEM((2, 2 * chunks, 2 * side, LANES), f32),
            pltpu.VMEM((2, 2 * chunks, 2 * side, LANES), f32),
            pltpu.VMEM((2, chunks, side, LANES), f32),
            pltpu.VMEM((4, 2 * quarter, side), bf16),
            pltpu.VMEM((4, 2 * quarter, side), f32),
            pltpu.VMEM((4, 2 * quarter, side), bf16),
            pltpu.VMEM((2, side, side), bf16),
            pltpu.VMEM((4, 2 * quarter, side), bf16),
            pltpu.VMEM((chunks, side, LANES), f32),
            pltpu.VMEM((2, chunks, side, LANES), f32),
            pltpu.VMEM((slots, side, side), bf16),
            *[pltpu.VMEM(tables[k].shape, bf16) for k in (0, 4, 1, 2, 3)],
            pltpu.SemaphoreType.DMA((4 * chunks,)),
            pltpu.SemaphoreType.DMA((slots,)),
            pltpu.SemaphoreType.DMA((5,)),
        ],
        compiler_params=pltpu.CompilerParams(vmem_limit_bytes=44 * 2**20),
        name="slots",
    )(counts, offset_y, offset_x, scale, obj_re, obj_im, right, *below, *diag, probe_re, probe_im, amplitude, *tables)
    parts = len(out_parts)
    return results[0], results[1], results[2:6], results[6 : 6 + parts], results[6 + parts :]


def finish_kernel(parts, *refs):
    own_ref, right_ref = refs[:2]
    below_refs = refs[2 : 2 + len(parts)]
    up_ref, far_ref, down_ref, low_ref, left_ref, beside_ref, out_re, out_im, cells, spill, result, ring_ref = refs[
        2 + len(parts) :
    ]
    side = own_ref.shape[1]
    chunks = side // LANES
    f32 = jnp.float32
    pad, count = 16, 8
    rows = chunks + 2
    for p in range(2):
        for k, column in enumerate((left_ref, beside_ref)):
            for a in range(chunks):
                lanes = slice(a * LANES, (a + 1) * LANES)
                at = rows + k * chunks + a
                ring_ref[2 * k + p : 2 * k + p + 1, lanes] = column[p : p + 1, lanes] + up_ref[p, at : at + 1, :]
    ring = ring_ref[...].T
    for p in range(2):
        for a in range(chunks):
            lanes = slice(a * LANES, (a + 1) * LANES)
            at = 0
            for rows, below_ref in zip(parts, below_refs):
                mine = slice(at, at + rows)
                cells[p, a + 1, pad + at : pad + at + rows, :] = (
                    own_ref[p, mine, lanes] + right_ref[p, mine, lanes].astype(f32) + below_ref[p, :, lanes].astype(f32)
                )
                at += rows
        for k in range(2):
            beside = jnp.broadcast_to(ring[:, 2 * k + p : 2 * k + p + 1], (side, LANES))
            cells[p, k * (chunks + 1), pad : pad + side, :] = beside
        for a in range(chunks + 2):
            one = slice(a, a + 1)
            cells[p, a, pad - 1 : pad, :] = up_ref[p, one, :] + far_ref[p, one, :]
            cells[p, a, pad + side : pad + side + 1, :] = down_ref[p, one, :] + low_ref[p, one, :]

    bound = 2.0 * shrink_level
    lane = lax.broadcasted_iota(jnp.int32, (count, LANES), 1)
    even, first, last = lane % 2 == 0, lane == 0, lane == LANES - 1
    cut = lambda t: jnp.clip(t, -bound, bound)
    later = lambda t: pltpu.roll(t, 1, axis=1)
    sooner = lambda t: pltpu.roll(t, LANES - 1, axis=1)

    def clips(total, gap, total_x, gap_x):
        side_by_side = cut(total - total_x)
        other = cut(gap + gap_x) + cut(gap - gap_x)
        return side_by_side + other, side_by_side - other

    def moved(p, at):
        upper = pl.ds(pad + 1 + 2 * at, count, stride=2)
        lower = pl.ds(pad + 2 + 2 * at, count, stride=2)
        high = [cells[p, a, upper, :] for a in range(chunks + 2)]
        low = [cells[p, a, lower, :] for a in range(chunks + 2)]
        fields = [[h + w for h, w in zip(high, low)], [h - w for h, w in zip(high, low)]]
        turned = []
        for field in fields:
            right_of = [later(field[a]) for a in range(chunks + 1)]
            left_of = [sooner(field[a]) for a in range(1, chunks + 2)]
            turned.append(
                [
                    jnp.where(
                        even,
                        jnp.where(first, right_of[a - 1], right_of[a]),
                        jnp.where(last, left_of[a], left_of[a - 1]),
                    )
                    for a in range(1, chunks + 1)
                ]
            )
        return [clips(fields[0][a + 1], fields[1][a + 1], turned[0][a], turned[1][a]) for a in range(chunks)]

    for p in range(2):
        for a, (_, below_one) in enumerate(moved(p, -count)):
            spill[p, a, 1 : 1 + count, :] = below_one

    def block(i, carry):
        at = pl.multiple_of(i * count, count)
        for p in range(2):
            shifted_clips = moved(p, at)
            for a in range(chunks):
                upper = pl.ds(pad + 2 * at, count, stride=2)
                lower = pl.ds(pad + 1 + 2 * at, count, stride=2)
                high, low = cells[p, a + 1, upper, :], cells[p, a + 1, lower, :]
                total, gap = high + low, high - low
                total_x = jnp.where(even, sooner(total), later(total))
                gap_x = jnp.where(even, sooner(gap), later(gap))
                top_clip, low_clip = clips(total, gap, total_x, gap_x)
                spill[p, a, pl.ds(at + count + 1, count), :] = shifted_clips[a][1]
                top_clip += spill[p, a, pl.ds(at + count, count), :]
                low_clip += shifted_clips[a][0]
                result[p, a, pl.ds(2 * at, count, stride=2), :] = high - 0.125 * top_clip
                result[p, a, pl.ds(2 * at + 1, count, stride=2), :] = low - 0.125 * low_clip
            for a in range(chunks):
                mine = pl.ds(2 * at, 2 * count)
                (out_re, out_im)[p][mine, a * LANES : (a + 1) * LANES] = result[p, a, mine, :]
        return carry

    lax.fori_loop(0, side // (2 * count), block, 0, unroll=UNROLL)


def run_finish(own, right, below, *edges):
    side = own.shape[1]
    chunks = side // LANES
    f32 = jnp.float32
    vmem = pl.BlockSpec(memory_space=pltpu.VMEM)
    tile = jax.ShapeDtypeStruct((side, side), f32)
    parts = [part.shape[1] for part in below]
    return pl.pallas_call(
        functools.partial(finish_kernel, parts),
        out_shape=(tile, tile),
        in_specs=[vmem] * (2 + len(parts) + len(edges)),
        out_specs=[vmem] * 2,
        scratch_shapes=[
            pltpu.VMEM((2, chunks + 2, side + 32, LANES), f32),
            pltpu.VMEM((2, chunks, side // 2 + 16, LANES), f32),
            pltpu.VMEM((2, chunks, side, LANES), f32),
            pltpu.VMEM((8, side), f32),
        ],
        compiler_params=pltpu.CompilerParams(vmem_limit_bytes=20 * 2**20),
        name="finish",
    )(own, right, *below, *edges)


def ring_kernel(right_ref, left_ref, second_ref, kept_ref, far_out, down_out, up_out, low_out, beside_left, beside_right):
    side = right_ref.shape[1] // 2
    chunks = side // LANES
    both = slice(0, 2 * side)
    beside_left[...] = left_ref[:, both] + second_ref[...]
    beside_right[...] = right_ref[...] + kept_ref[:, both]
    for k, (target, at) in enumerate(((up_out, 0), (down_out, side - 1), (low_out, side), (far_out, 2 * side - 1))):
        for p in range(2):
            here = slice(p, p + 1)
            for row, column in ((0, beside_left), (chunks + 1, beside_right)):
                target[p, row : row + 1, :] = jnp.broadcast_to(column[here, at : at + 1], (1, LANES))
            for a in range(chunks):
                lanes = slice(2 * side + k * side + a * LANES, 2 * side + k * side + (a + 1) * LANES)
                target[p, a + 1 : a + 2, :] = kept_ref[here, lanes] + left_ref[here, lanes]
    for p in range(2):
        for k, column in enumerate((beside_left, beside_right)):
            for a in range(chunks):
                row = chunks + 2 + k * chunks + a
                lanes = slice(side + a * LANES, side + (a + 1) * LANES)
                down_out[p, row : row + 1, :] = column[p : p + 1, lanes]


def run_ring(right, left, second, kept):
    wide = right.shape[1]
    chunks = wide // 2 // LANES
    vmem = pl.BlockSpec(memory_space=pltpu.VMEM)
    rows = [chunks + 2, 3 * chunks + 2, chunks + 2, chunks + 2]
    shapes = [(2, n, LANES) for n in rows] + [(2, wide)] * 2
    return pl.pallas_call(
        ring_kernel,
        out_shape=[jax.ShapeDtypeStruct(shape, jnp.float32) for shape in shapes],
        in_specs=[vmem] * 4,
        out_specs=[vmem] * 6,
        compiler_params=pltpu.CompilerParams(vmem_limit_bytes=2 * 2**20),
        name="ring",
    )(right, left, second, kept)


def shifted(value, axis, steps):
    count = lax.axis_size(axis)
    return lax.ppermute(value, axis, [(i, (i + steps) % count) for i in range(count)])


def parts_of(side, weights):
    unit = side // 32
    sizes = [unit * weight for weight in weights]
    assert sum(sizes) == side and unit % 16 == 0
    return sizes


def split_rows(value, sizes):
    ends = np.cumsum(sizes)
    return [value[:, end - size : end] for end, size in zip(ends, sizes)]


def update(obj_re, obj_im, probe_re, probe_im, amplitude, offset_y, offset_x, counts):
    f32, bf16 = jnp.float32, jnp.bfloat16
    side = probe_re.shape[0]
    in_parts, out_parts = parts_of(side, IN_SHARES), parts_of(side, OUT_SHARES)

    head = in_parts[0]
    piece = jnp.stack([obj_re[:head], obj_im[:head]]).astype(bf16)
    piece, later_re, later_im = lax.optimization_barrier((piece, obj_re, obj_im))
    below = [shifted(piece, "row", -1)]
    own = jnp.stack([later_re, later_im]).astype(bf16)
    right = shifted(own, "col", -1)
    for rest in split_rows(own, in_parts)[1:]:
        below.append(shifted(rest, "row", -1))
    diag = [shifted(value, "col", -1) for value in below]
    probe_power = jnp.mean(probe_re * probe_re + probe_im * probe_im) + epsilon
    scale = (step_size / probe_power).reshape(1, 1)
    own_sum, right_sum, edges, below_sum, diag_sum = run_slots(
        counts, offset_y, offset_x, scale, obj_re, obj_im, right, below, diag, probe_re, probe_im, amplitude, out_parts
    )

    to_left, to_right, kept, to_second = edges
    diag_in = [shifted(value, "col", 1) for value in diag_sum]
    ring_parts = (shifted(to_left, "col", -1), shifted(to_right, "col", 1), shifted(to_second, "col", 2))
    right_in = shifted(right_sum, "col", 1)
    below_in = []
    for mine, theirs in zip(below_sum, diag_in):
        sent = (mine + theirs.astype(f32)).astype(bf16)
        below_in.append(shifted(sent, "row", 1))
    low_last, sent_down, first, low_first, beside_left, beside_right = run_ring(*ring_parts, kept)
    from_far = shifted(low_last, "row", 2)
    from_up = shifted(sent_down, "row", 1)
    from_down = shifted(first, "row", -1)
    return run_finish(own_sum, right_in, below_in, from_up, from_far, from_down, low_first, beside_left, beside_right)


IN_SHARES = (16, 8, 5, 3)
OUT_SHARES = (4, 12, 16)


def solution(mesh):
    split = P("row", "col")
    return jax.shard_map(
        update,
        mesh=mesh,
        in_specs=(split, split, P(), P(), P("row", "col", None, None), split, split, split),
        out_specs=(split, split),
        check_vma=False,
    )
```

```python
import functools
import math

import jax
import jax.numpy as jnp
import numpy as np
from jax import lax
from jax.experimental import pallas as pl
from jax.experimental.pallas import tpu as pltpu
from jax.sharding import PartitionSpec as P


modulus_floor = 0.5
shrink_level = 0.2
step_size = 0.5
epsilon = 1e-05
LANES = 128
UNROLL = 4


def transform_tables(side):
    quarter, half = side // 4, side // 2
    bf16 = jnp.bfloat16

    def cos_sin(rows, cols):
        angle = (rows[:, None] * cols[None, :] % side) * (2.0 * math.pi / side)
        norm = 1.0 / math.sqrt(side)
        return np.cos(angle) * norm, -np.sin(angle) * norm

    base = np.arange(quarter)
    grouped = np.concatenate([base[c::4] for c in range(4)])
    rows_in, rows_out = [], []
    for c in range(4):
        members = 4 * base + c
        co, si = cos_sin(grouped, members)
        rows_in.append(np.block([[co, -si], [si, co]]))
        co, si = cos_sin(base, members)
        rows_out.append(np.block([[co, si], [-si, co]]))
    frequency = np.concatenate([np.arange(0, half, 2), np.arange(1, half, 2)])
    mirrored = (side - frequency) % side
    mirrored[0] = half
    every = np.arange(side)
    co, si = cos_sin(every, frequency)
    co[:, 0] = np.where(every % 2 == 0, co[:, 0], 0.0)
    si[:, 0] = np.where(every % 2 == 1, 1.0 / math.sqrt(side), 0.0)
    cols_in = np.concatenate([co, si], axis=1)
    cols_out = []
    for part in range(2):
        run = slice(part * quarter, (part + 1) * quarter)
        members = np.concatenate([frequency[run], mirrored[run]])
        co, si = cos_sin(members, np.arange(half))
        cols_out.append(np.block([[co, -si], [si, co]]))
    order = np.concatenate([frequency, mirrored])
    pick = np.zeros((side, side))
    pick[order, every] = 1.0
    return tuple(
        np.asarray(np.asarray(table, np.float32), dtype=bf16)
        for table in (np.stack(rows_in), cols_in, np.stack(cols_out), np.stack(rows_out), pick)
    )


def dot(left_op, right_op):
    return jnp.dot(left_op, right_op, preferred_element_type=jnp.float32)


def slots_kernel(side, in_parts, out_parts, *refs):
    refs = list(refs)

    def take(count):
        taken = refs[:count]
        del refs[:count]
        return taken

    count_ref, oy_ref, ox_ref, scale_ref, own_re, own_im, right_ref = take(7)
    below_refs, diag_refs = take(len(in_parts)), take(len(in_parts))
    probe_re, probe_im, amp_ref = take(3)
    rows_in, cols_in, cols_out, rows_out, pick = take(5)
    own_out, right_out, left_out, beside_out, kept_out, second_out = take(6)
    below_outs, diag_outs = take(len(out_parts)), take(len(out_parts))
    region, sums, probe, exits, wide, half, delta, back, amp, held, amp_held, wave = refs[:12]
    table_held, sems, amp_sems, table_sems = refs[12:17], refs[17], refs[18], refs[19]
    quarter, chunks = side // 4, side // LANES
    f32, bf16 = jnp.float32, jnp.bfloat16

    def fetches(sources, target, at):
        return [
            pltpu.make_async_copy(
                sources[p].at[:, a * LANES : (a + 1) * LANES], target.at[p, a], sems.at[at + p * chunks + a]
            )
            for p in range(2)
            for a in range(chunks)
        ]

    def amp_fetch(s):
        return pltpu.make_async_copy(amp_ref.at[0, s], amp_held.at[s], amp_sems.at[s])

    own_copies = fetches((own_re, own_im), held, 0)
    late_copies = fetches((probe_re, probe_im), probe, 2 * chunks)
    tables = (rows_in, pick, cols_in, cols_out, rows_out)
    late_copies += [
        pltpu.make_async_copy(table, target, table_sems.at[k]) for k, (table, target) in enumerate(zip(tables, table_held))
    ]
    for copy in own_copies + late_copies:
        copy.start()

    def start_amp(s, carry):
        amp_fetch(s).start()
        return carry

    lax.fori_loop(0, count_ref[0, 0], start_amp, 0)
    rows_in, pick, cols_in, cols_out, rows_out = table_held
    sums[...] = jnp.zeros_like(sums)

    for p in range(2):
        for a in range(chunks):
            lanes = slice(a * LANES, (a + 1) * LANES)
            region[p, chunks + a, :side, :] = right_ref[p, :, lanes].astype(f32)
            at = side
            for rows, below_ref, diag_ref in zip(in_parts, below_refs, diag_refs):
                region[p, a, at : at + rows, :] = below_ref[p, :, lanes].astype(f32)
                region[p, chunks + a, at : at + rows, :] = diag_ref[p, :, lanes].astype(f32)
                at += rows
    for copy in own_copies:
        copy.wait()
    for p in range(2):
        for a in range(chunks):
            region[p, a, :side, :] = held[p, a].astype(bf16).astype(f32)
    for copy in late_copies:
        copy.wait()

    lane = lax.broadcasted_iota(jnp.int32, (1, LANES), 1)

    def corner(s):
        return oy_ref[0, s], ox_ref[0, s] // LANES, ox_ref[0, s] % LANES

    def take_patch(s, c):
        oy, q, b = corner(s)
        rows = pl.ds(oy + c, quarter, stride=4)
        mine = pl.ds(c, quarter, stride=4)
        before = None
        for a in range(chunks + 1):
            now = [pltpu.roll(region[p, q + a, rows, :], (LANES - b) % LANES, axis=1) for p in range(2)]
            if a > 0:
                o_re, o_im = (jnp.where(lane < LANES - b, before[p], now[p]) for p in range(2))
                p_re, p_im = probe[0, a - 1, mine, :], probe[1, a - 1, mine, :]
                lanes = slice((a - 1) * LANES, a * LANES)
                exits[c, :quarter, lanes] = (p_re * o_re - p_im * o_im).astype(bf16)
                exits[c, quarter:, lanes] = (p_re * o_im + p_im * o_re).astype(bf16)
            before = now

    rows_at = 16

    def place_term(s, r):
        oy, q, b = corner(s)
        at = r * rows_at
        before = [jnp.zeros((rows_at, LANES), f32)] * 8
        for a in range(chunks + 1):
            now = [jnp.zeros((rows_at, LANES), f32)] * 8
            if a < chunks:
                lanes = slice(a * LANES, (a + 1) * LANES)
                re = [wave[c, at : at + rows_at, lanes] for c in range(4)]
                im = [wave[c, quarter + at : quarter + at + rows_at, lanes] for c in range(4)]
                er, ei, fr, fi = re[0] + re[2], im[0] + im[2], re[0] - re[2], im[0] - im[2]
                gr, gi, hr, hi = re[1] + re[3], im[1] + im[3], re[1] - re[3], im[1] - im[3]
                outs = ((er + gr, ei + gi), (fr - hi, fi + hr), (er - gr, ei - gi), (fr + hi, fi - hr))
                for m, (w_re, w_im) in enumerate(outs):
                    mine = slice(m * quarter + at, m * quarter + at + rows_at)
                    p_re, p_im = probe[0, a, mine, :], probe[1, a, mine, :]
                    now[2 * m] = pltpu.roll(p_re * w_re + p_im * w_im, b, axis=1)
                    now[2 * m + 1] = pltpu.roll(p_re * w_im - p_im * w_re, b, axis=1)
            for k in range(8):
                rows = pl.ds(oy + (k // 2) * quarter + at, rows_at)
                sums[k % 2, q + a, rows, :] += jnp.where(lane >= b, now[k], before[k])
            before = now

    blocks = quarter // rows_at
    wave[...] = jnp.zeros_like(wave)
    for c in range(4):
        take_patch(0, c)

    def one_slot(s, carry):
        later, earlier = jnp.minimum(s + 1, amp_held.shape[0] - 1), jnp.maximum(s - 1, 0)
        amp_fetch(s).wait()
        for c in range(4):
            wide[c] = dot(rows_in[c], exits[c])
        step = quarter // 4
        for cc in range(4):
            for a in range(chunks):
                lanes = slice(a * LANES, (a + 1) * LANES)
                re = [wide[c, cc * step : (cc + 1) * step, lanes] for c in range(4)]
                im = [wide[c, quarter + cc * step : quarter + (cc + 1) * step, lanes] for c in range(4)]
                er, ei, fr, fi = re[0] + re[2], im[0] + im[2], re[0] - re[2], im[0] - im[2]
                gr, gi, hr, hi = re[1] + re[3], im[1] + im[3], re[1] - re[3], im[1] - im[3]
                outs = (
                    (er + gr, ei + gi),
                    (fr + hi, fi - hr),
                    (er - gr, ei - gi),
                    (fr - hi, fi + hr),
                )
                for m, (o_re, o_im) in enumerate(outs):
                    half[cc, m * step : (m + 1) * step, lanes] = o_re.astype(bf16)
                    half[cc, quarter + m * step : quarter + (m + 1) * step, lanes] = o_im.astype(bf16)

        ordered = dot(amp_held[s], pick[...])
        for a in range(chunks):
            amp[a] = ordered[:, a * LANES : (a + 1) * LANES]

        for cc in range(4):
            wide[cc] = dot(half[cc], cols_in[...])
            take_patch(later, cc)
        mid = chunks // 2
        for cc in range(4):
            for part in range(mid):
                lo = slice(part * LANES, (part + 1) * LANES)
                hi = slice((mid + part) * LANES, (mid + part + 1) * LANES)
                p1, p3 = wide[cc, :quarter, lo], wide[cc, :quarter, hi]
                p4, p2 = wide[cc, quarter:, lo], wide[cc, quarter:, hi]
                if part == 0:
                    p2, p3 = jnp.where(lane == 0, -p3, p2), jnp.where(lane == 0, p2, p3)
                for sign in range(2):
                    s_re = p1 - p2 if sign == 0 else p1 + p2
                    s_im = p4 + p3 if sign == 0 else p4 - p3
                    measured = amp[sign * mid + part, pl.ds(cc, quarter, stride=4), :]
                    inverse = jnp.minimum(lax.rsqrt(s_re * s_re + s_im * s_im), 1.0 / modulus_floor)
                    factor = measured * inverse - 1.0
                    rows = slice(cc * quarter, (cc + 1) * quarter)
                    for k, value in ((sign, s_re), (2 + sign, s_im)):
                        delta[part, rows, k * LANES : (k + 1) * LANES] = (value * factor).astype(bf16)

        for part in range(2):
            for r in range(2):
                wide[2 * part + r] = dot(delta[part, r * side // 2 : (r + 1) * side // 2, :], cols_out[part])
                for block in range(blocks // 4):
                    place_term(earlier, (2 * part + r) * (blocks // 4) + block)
        for cc in range(4):
            for k in range(2):
                for a in range(mid):
                    lanes = slice((k * mid + a) * LANES, (k * mid + a + 1) * LANES)
                    rows = slice((cc % 2) * quarter, (cc % 2 + 1) * quarter)
                    even, odd = wide[cc // 2, rows, lanes], wide[2 + cc // 2, rows, lanes]
                    put = slice(k * quarter, (k + 1) * quarter)
                    back[cc, put, a * LANES : (a + 1) * LANES] = (even + odd).astype(bf16)
                    back[cc, put, (mid + a) * LANES : (mid + a + 1) * LANES] = (even - odd).astype(bf16)

        for c in range(4):
            wave[c] = dot(rows_out[c], back[c])
        return carry

    lax.fori_loop(0, count_ref[0, 0], one_slot, 0)
    for r in range(blocks):
        place_term(count_ref[0, 0] - 1, r)

    scale = scale_ref[0, 0]
    for p in range(2):
        for a in range(chunks):
            lanes = slice(a * LANES, (a + 1) * LANES)
            right_out[p, :, lanes] = (scale * sums[p, chunks + a, :side, :]).astype(bf16)
            own_out[p, :, lanes] = held[p, a] + scale * sums[p, a, :side, :]
            at = side
            for rows, below_out, diag_out in zip(out_parts, below_outs, diag_outs):
                below_out[p, :, lanes] = scale * sums[p, a, at : at + rows, :]
                diag_out[p, :, lanes] = (scale * sums[p, chunks + a, at : at + rows, :]).astype(bf16)
                at += rows
        here = slice(p, p + 1)
        columns = (
            (left_out, 0, 0, True),
            (beside_out, chunks - 1, LANES - 1, True),
            (kept_out, chunks, 0, False),
            (second_out, 2 * chunks - 1, LANES - 1, False),
        )
        for target, a, at, with_own in columns:
            cells = scale * sums[p, a]
            turned = jnp.concatenate([cells[r * LANES : (r + 1) * LANES, :].T[at : at + 1, :] for r in range(2 * chunks)], axis=1)
            if with_own:
                own_turned = [held[p, a, r * LANES : (r + 1) * LANES, :].T[at : at + 1, :] for r in range(chunks)]
                turned += jnp.concatenate(own_turned + [jnp.zeros((1, side), f32)], axis=1)
            target[here, : 2 * side] = turned
        for k, row in enumerate((0, side - 1, side, 2 * side - 1)):
            for a in range(chunks):
                at = 2 * side + k * side + a * LANES
                mine = scale * sums[p, a, row : row + 1, :]
                if k < 2:
                    mine += held[p, a, row : row + 1, :]
                kept_out[here, at : at + LANES] = mine
                beside_out[here, at : at + LANES] = scale * sums[p, chunks + a, row : row + 1, :]


def run_slots(counts, offset_y, offset_x, scale, obj_re, obj_im, right, below, diag, probe_re, probe_im, amplitude, out_parts):
    side = probe_re.shape[0]
    chunks, quarter = side // LANES, side // 4
    f32, bf16 = jnp.float32, jnp.bfloat16
    tables = transform_tables(side)
    in_parts = [part.shape[1] for part in below]
    smem = pl.BlockSpec(memory_space=pltpu.SMEM)
    vmem = pl.BlockSpec(memory_space=pltpu.VMEM)
    here = pl.BlockSpec(memory_space=pl.ANY)
    slots = amplitude.shape[1]
    tile = lambda rows, kind: jax.ShapeDtypeStruct((2, rows, side), kind)
    outs = [tile(side, f32), tile(side, bf16)] + [jax.ShapeDtypeStruct((2, n * side), f32) for n in (2, 6, 6, 2)]
    outs += [tile(rows, f32) for rows in out_parts] + [tile(rows, bf16) for rows in out_parts]
    results = pl.pallas_call(
        functools.partial(slots_kernel, side, in_parts, out_parts),
        out_shape=outs,
        in_specs=[smem] * 4 + [here] * 2 + [vmem] * (1 + 2 * len(in_parts)) + [here] * 8,
        out_specs=[vmem] * len(outs),
        scratch_shapes=[
            pltpu.VMEM((2, 2 * chunks, 2 * side, LANES), f32),
            pltpu.VMEM((2, 2 * chunks, 2 * side, LANES), f32),
            pltpu.VMEM((2, chunks, side, LANES), f32),
            pltpu.VMEM((4, 2 * quarter, side), bf16),
            pltpu.VMEM((4, 2 * quarter, side), f32),
            pltpu.VMEM((4, 2 * quarter, side), bf16),
            pltpu.VMEM((2, side, side), bf16),
            pltpu.VMEM((4, 2 * quarter, side), bf16),
            pltpu.VMEM((chunks, side, LANES), f32),
            pltpu.VMEM((2, chunks, side, LANES), f32),
            pltpu.VMEM((slots, side, side), bf16),
            pltpu.VMEM((4, 2 * quarter, side), f32),
            *[pltpu.VMEM(tables[k].shape, bf16) for k in (0, 4, 1, 2, 3)],
            pltpu.SemaphoreType.DMA((4 * chunks,)),
            pltpu.SemaphoreType.DMA((slots,)),
            pltpu.SemaphoreType.DMA((5,)),
        ],
        compiler_params=pltpu.CompilerParams(vmem_limit_bytes=46 * 2**20),
        name="slots",
    )(counts, offset_y, offset_x, scale, obj_re, obj_im, right, *below, *diag, probe_re, probe_im, amplitude, *tables)
    parts = len(out_parts)
    return results[0], results[1], results[2:6], results[6 : 6 + parts], results[6 + parts :]


def finish_kernel(parts, *refs):
    own_ref, right_ref = refs[:2]
    below_refs = refs[2 : 2 + len(parts)]
    up_ref, far_ref, down_ref, low_ref, left_ref, beside_ref, out_re, out_im, cells, spill, result, ring_ref = refs[
        2 + len(parts) :
    ]
    side = own_ref.shape[1]
    chunks = side // LANES
    f32 = jnp.float32
    pad, count = 16, 8
    rows = chunks + 2
    for p in range(2):
        for k, column in enumerate((left_ref, beside_ref)):
            for a in range(chunks):
                lanes = slice(a * LANES, (a + 1) * LANES)
                at = rows + k * chunks + a
                ring_ref[2 * k + p : 2 * k + p + 1, lanes] = column[p : p + 1, lanes] + up_ref[p, at : at + 1, :]
    ring = ring_ref[...].T
    for p in range(2):
        for a in range(chunks):
            lanes = slice(a * LANES, (a + 1) * LANES)
            at = 0
            for rows, below_ref in zip(parts, below_refs):
                mine = slice(at, at + rows)
                cells[p, a + 1, pad + at : pad + at + rows, :] = (
                    own_ref[p, mine, lanes] + right_ref[p, mine, lanes].astype(f32) + below_ref[p, :, lanes].astype(f32)
                )
                at += rows
        for k in range(2):
            beside = jnp.broadcast_to(ring[:, 2 * k + p : 2 * k + p + 1], (side, LANES))
            cells[p, k * (chunks + 1), pad : pad + side, :] = beside
        for a in range(chunks + 2):
            one = slice(a, a + 1)
            cells[p, a, pad - 1 : pad, :] = up_ref[p, one, :] + far_ref[p, one, :]
            cells[p, a, pad + side : pad + side + 1, :] = down_ref[p, one, :] + low_ref[p, one, :]

    bound = 2.0 * shrink_level
    lane = lax.broadcasted_iota(jnp.int32, (count, LANES), 1)
    even, first, last = lane % 2 == 0, lane == 0, lane == LANES - 1
    cut = lambda t: jnp.clip(t, -bound, bound)
    later = lambda t: pltpu.roll(t, 1, axis=1)
    sooner = lambda t: pltpu.roll(t, LANES - 1, axis=1)

    def clips(total, gap, total_x, gap_x):
        side_by_side = cut(total - total_x)
        other = cut(gap + gap_x) + cut(gap - gap_x)
        return side_by_side + other, side_by_side - other

    def moved(p, at):
        upper = pl.ds(pad + 1 + 2 * at, count, stride=2)
        lower = pl.ds(pad + 2 + 2 * at, count, stride=2)
        high = [cells[p, a, upper, :] for a in range(chunks + 2)]
        low = [cells[p, a, lower, :] for a in range(chunks + 2)]
        fields = [[h + w for h, w in zip(high, low)], [h - w for h, w in zip(high, low)]]
        turned = []
        for field in fields:
            right_of = [later(field[a]) for a in range(chunks + 1)]
            left_of = [sooner(field[a]) for a in range(1, chunks + 2)]
            turned.append(
                [
                    jnp.where(
                        even,
                        jnp.where(first, right_of[a - 1], right_of[a]),
                        jnp.where(last, left_of[a], left_of[a - 1]),
                    )
                    for a in range(1, chunks + 1)
                ]
            )
        return [clips(fields[0][a + 1], fields[1][a + 1], turned[0][a], turned[1][a]) for a in range(chunks)]

    for p in range(2):
        for a, (_, below_one) in enumerate(moved(p, -count)):
            spill[p, a, 1 : 1 + count, :] = below_one

    def block(i, carry):
        at = pl.multiple_of(i * count, count)
        for p in range(2):
            shifted_clips = moved(p, at)
            for a in range(chunks):
                upper = pl.ds(pad + 2 * at, count, stride=2)
                lower = pl.ds(pad + 1 + 2 * at, count, stride=2)
                high, low = cells[p, a + 1, upper, :], cells[p, a + 1, lower, :]
                total, gap = high + low, high - low
                total_x = jnp.where(even, sooner(total), later(total))
                gap_x = jnp.where(even, sooner(gap), later(gap))
                top_clip, low_clip = clips(total, gap, total_x, gap_x)
                spill[p, a, pl.ds(at + count + 1, count), :] = shifted_clips[a][1]
                top_clip += spill[p, a, pl.ds(at + count, count), :]
                low_clip += shifted_clips[a][0]
                result[p, a, pl.ds(2 * at, count, stride=2), :] = high - 0.125 * top_clip
                result[p, a, pl.ds(2 * at + 1, count, stride=2), :] = low - 0.125 * low_clip
            for a in range(chunks):
                mine = pl.ds(2 * at, 2 * count)
                (out_re, out_im)[p][mine, a * LANES : (a + 1) * LANES] = result[p, a, mine, :]
        return carry

    lax.fori_loop(0, side // (2 * count), block, 0, unroll=UNROLL)


def run_finish(own, right, below, *edges):
    side = own.shape[1]
    chunks = side // LANES
    f32 = jnp.float32
    vmem = pl.BlockSpec(memory_space=pltpu.VMEM)
    tile = jax.ShapeDtypeStruct((side, side), f32)
    parts = [part.shape[1] for part in below]
    return pl.pallas_call(
        functools.partial(finish_kernel, parts),
        out_shape=(tile, tile),
        in_specs=[vmem] * (2 + len(parts) + len(edges)),
        out_specs=[vmem] * 2,
        scratch_shapes=[
            pltpu.VMEM((2, chunks + 2, side + 32, LANES), f32),
            pltpu.VMEM((2, chunks, side // 2 + 16, LANES), f32),
            pltpu.VMEM((2, chunks, side, LANES), f32),
            pltpu.VMEM((8, side), f32),
        ],
        compiler_params=pltpu.CompilerParams(vmem_limit_bytes=20 * 2**20),
        name="finish",
    )(own, right, *below, *edges)


def ring_kernel(right_ref, left_ref, second_ref, kept_ref, far_out, down_out, up_out, low_out, beside_left, beside_right):
    side = right_ref.shape[1] // 2
    chunks = side // LANES
    both = slice(0, 2 * side)
    beside_left[...] = left_ref[:, both] + second_ref[...]
    beside_right[...] = right_ref[...] + kept_ref[:, both]
    for k, (target, at) in enumerate(((up_out, 0), (down_out, side - 1), (low_out, side), (far_out, 2 * side - 1))):
        for p in range(2):
            here = slice(p, p + 1)
            for row, column in ((0, beside_left), (chunks + 1, beside_right)):
                target[p, row : row + 1, :] = jnp.broadcast_to(column[here, at : at + 1], (1, LANES))
            for a in range(chunks):
                lanes = slice(2 * side + k * side + a * LANES, 2 * side + k * side + (a + 1) * LANES)
                target[p, a + 1 : a + 2, :] = kept_ref[here, lanes] + left_ref[here, lanes]
    for p in range(2):
        for k, column in enumerate((beside_left, beside_right)):
            for a in range(chunks):
                row = chunks + 2 + k * chunks + a
                lanes = slice(side + a * LANES, side + (a + 1) * LANES)
                down_out[p, row : row + 1, :] = column[p : p + 1, lanes]


def run_ring(right, left, second, kept):
    wide = right.shape[1]
    chunks = wide // 2 // LANES
    vmem = pl.BlockSpec(memory_space=pltpu.VMEM)
    rows = [chunks + 2, 3 * chunks + 2, chunks + 2, chunks + 2]
    shapes = [(2, n, LANES) for n in rows] + [(2, wide)] * 2
    return pl.pallas_call(
        ring_kernel,
        out_shape=[jax.ShapeDtypeStruct(shape, jnp.float32) for shape in shapes],
        in_specs=[vmem] * 4,
        out_specs=[vmem] * 6,
        compiler_params=pltpu.CompilerParams(vmem_limit_bytes=2 * 2**20),
        name="ring",
    )(right, left, second, kept)


def shifted(value, axis, steps):
    count = lax.axis_size(axis)
    return lax.ppermute(value, axis, [(i, (i + steps) % count) for i in range(count)])


def parts_of(side, weights):
    unit = side // 32
    sizes = [unit * weight for weight in weights]
    assert sum(sizes) == side and unit % 16 == 0
    return sizes


def split_rows(value, sizes):
    ends = np.cumsum(sizes)
    return [value[:, end - size : end] for end, size in zip(ends, sizes)]


def update(obj_re, obj_im, probe_re, probe_im, amplitude, offset_y, offset_x, counts):
    f32, bf16 = jnp.float32, jnp.bfloat16
    side = probe_re.shape[0]
    in_parts, out_parts = parts_of(side, IN_SHARES), parts_of(side, OUT_SHARES)

    head = in_parts[0]
    piece = jnp.stack([obj_re[:head], obj_im[:head]]).astype(bf16)
    piece, later_re, later_im = lax.optimization_barrier((piece, obj_re, obj_im))
    below = [shifted(piece, "row", -1)]
    own = jnp.stack([later_re, later_im]).astype(bf16)
    right = shifted(own, "col", -1)
    for rest in split_rows(own, in_parts)[1:]:
        below.append(shifted(rest, "row", -1))
    diag = [shifted(value, "col", -1) for value in below]
    probe_power = jnp.mean(probe_re * probe_re + probe_im * probe_im) + epsilon
    scale = (step_size / probe_power).reshape(1, 1)
    own_sum, right_sum, edges, below_sum, diag_sum = run_slots(
        counts, offset_y, offset_x, scale, obj_re, obj_im, right, below, diag, probe_re, probe_im, amplitude, out_parts
    )

    to_left, to_right, kept, to_second = edges
    diag_in = [shifted(value, "col", 1) for value in diag_sum]
    ring_parts = (shifted(to_left, "col", -1), shifted(to_right, "col", 1), shifted(to_second, "col", 2))
    right_in = shifted(right_sum, "col", 1)
    below_in = []
    for mine, theirs in zip(below_sum, diag_in):
        sent = (mine + theirs.astype(f32)).astype(bf16)
        below_in.append(shifted(sent, "row", 1))
    low_last, sent_down, first, low_first, beside_left, beside_right = run_ring(*ring_parts, kept)
    from_far = shifted(low_last, "row", 2)
    from_up = shifted(sent_down, "row", 1)
    from_down = shifted(first, "row", -1)
    return run_finish(own_sum, right_in, below_in, from_up, from_far, from_down, low_first, beside_left, beside_right)


IN_SHARES = (16, 8, 5, 3)
OUT_SHARES = (5, 9, 18)


def solution(mesh):
    split = P("row", "col")
    return jax.shard_map(
        update,
        mesh=mesh,
        in_specs=(split, split, P(), P(), P("row", "col", None, None), split, split, split),
        out_specs=(split, split),
        check_vma=False,
    )
```

```python
import functools
import math

import jax
import jax.numpy as jnp
import numpy as np
from jax import lax
from jax.experimental import pallas as pl
from jax.experimental.pallas import tpu as pltpu
from jax.sharding import PartitionSpec as P


modulus_floor = 0.5
shrink_level = 0.2
step_size = 0.5
epsilon = 1e-05
LANES = 128
UNROLL = 4


def transform_tables(side):
    quarter, half = side // 4, side // 2
    bf16 = jnp.bfloat16

    def cos_sin(rows, cols):
        angle = (rows[:, None] * cols[None, :] % side) * (2.0 * math.pi / side)
        norm = 1.0 / math.sqrt(side)
        return np.cos(angle) * norm, -np.sin(angle) * norm

    base = np.arange(quarter)
    grouped = np.concatenate([base[c::4] for c in range(4)])
    rows_in, rows_out = [], []
    for c in range(4):
        members = 4 * base + c
        co, si = cos_sin(grouped, members)
        rows_in.append(np.block([[co, -si], [si, co]]))
        co, si = cos_sin(base, members)
        rows_out.append(np.block([[co, si], [-si, co]]))
    frequency = np.concatenate([np.arange(0, half, 2), np.arange(1, half, 2)])
    mirrored = (side - frequency) % side
    mirrored[0] = half
    every = np.arange(side)
    co, si = cos_sin(every, frequency)
    co[:, 0] = np.where(every % 2 == 0, co[:, 0], 0.0)
    si[:, 0] = np.where(every % 2 == 1, 1.0 / math.sqrt(side), 0.0)
    cols_in = np.concatenate([co, si], axis=1)
    cols_out = []
    for part in range(2):
        run = slice(part * quarter, (part + 1) * quarter)
        members = np.concatenate([frequency[run], mirrored[run]])
        co, si = cos_sin(members, np.arange(half))
        cols_out.append(np.block([[co, -si], [si, co]]))
    order = np.concatenate([frequency, mirrored])
    pick = np.zeros((side, side))
    pick[order, every] = 1.0
    return tuple(
        np.asarray(np.asarray(table, np.float32), dtype=bf16)
        for table in (np.stack(rows_in), cols_in, np.stack(cols_out), np.stack(rows_out), pick)
    )


def dot(left_op, right_op):
    return jnp.dot(left_op, right_op, preferred_element_type=jnp.float32)


def slots_kernel(side, in_parts, out_parts, *refs):
    refs = list(refs)

    def take(count):
        taken = refs[:count]
        del refs[:count]
        return taken

    count_ref, oy_ref, ox_ref, scale_ref, own_re, own_im, right_ref = take(7)
    below_refs, diag_refs = take(len(in_parts)), take(len(in_parts))
    probe_re, probe_im, amp_ref = take(3)
    rows_in, cols_in, cols_out, rows_out = take(4)
    own_out, right_out, left_out, beside_out, kept_out, second_out = take(6)
    below_outs, diag_outs = take(len(out_parts)), take(len(out_parts))
    region, sums, probe, exits, wide, half, delta, back, held, amp_held, wave = refs[:11]
    table_held, sems, amp_sems, table_sems = refs[11:15], refs[15], refs[16], refs[17]
    quarter, chunks = side // 4, side // LANES
    f32, bf16 = jnp.float32, jnp.bfloat16

    def fetches(sources, target, at):
        return [
            pltpu.make_async_copy(
                sources[p].at[:, a * LANES : (a + 1) * LANES], target.at[p, a], sems.at[at + p * chunks + a]
            )
            for p in range(2)
            for a in range(chunks)
        ]

    def amp_fetch(s):
        return pltpu.make_async_copy(amp_ref.at[s], amp_held.at[s], amp_sems.at[s])

    own_copies = fetches((own_re, own_im), held, 0)
    late_copies = fetches((probe_re, probe_im), probe, 2 * chunks)
    tables = (rows_in, cols_in, cols_out, rows_out)
    late_copies += [
        pltpu.make_async_copy(table, target, table_sems.at[k]) for k, (table, target) in enumerate(zip(tables, table_held))
    ]
    for copy in own_copies + late_copies:
        copy.start()

    def start_amp(s, carry):
        amp_fetch(s).start()
        return carry

    lax.fori_loop(0, count_ref[0, 0], start_amp, 0)
    rows_in, cols_in, cols_out, rows_out = table_held
    sums[...] = jnp.zeros_like(sums)

    for p in range(2):
        for a in range(chunks):
            lanes = slice(a * LANES, (a + 1) * LANES)
            region[p, chunks + a, :side, :] = right_ref[p, :, lanes].astype(f32)
            at = side
            for rows, below_ref, diag_ref in zip(in_parts, below_refs, diag_refs):
                region[p, a, at : at + rows, :] = below_ref[p, :, lanes].astype(f32)
                region[p, chunks + a, at : at + rows, :] = diag_ref[p, :, lanes].astype(f32)
                at += rows
    for copy in own_copies:
        copy.wait()
    for p in range(2):
        for a in range(chunks):
            region[p, a, :side, :] = held[p, a].astype(bf16).astype(f32)
    for copy in late_copies:
        copy.wait()

    lane = lax.broadcasted_iota(jnp.int32, (1, LANES), 1)

    def corner(s):
        return oy_ref[0, s], ox_ref[0, s] // LANES, ox_ref[0, s] % LANES

    def take_patch(s, c):
        oy, q, b = corner(s)
        rows = pl.ds(oy + c, quarter, stride=4)
        mine = pl.ds(c, quarter, stride=4)
        before = None
        for a in range(chunks + 1):
            now = [pltpu.roll(region[p, q + a, rows, :], (LANES - b) % LANES, axis=1) for p in range(2)]
            if a > 0:
                o_re, o_im = (jnp.where(lane < LANES - b, before[p], now[p]) for p in range(2))
                p_re, p_im = probe[0, a - 1, mine, :], probe[1, a - 1, mine, :]
                lanes = slice((a - 1) * LANES, a * LANES)
                exits[c, :quarter, lanes] = (p_re * o_re - p_im * o_im).astype(bf16)
                exits[c, quarter:, lanes] = (p_re * o_im + p_im * o_re).astype(bf16)
            before = now

    rows_at = 16

    def place_term(s, r):
        oy, q, b = corner(s)
        at = r * rows_at
        before = [jnp.zeros((rows_at, LANES), f32)] * 8
        for a in range(chunks + 1):
            now = [jnp.zeros((rows_at, LANES), f32)] * 8
            if a < chunks:
                lanes = slice(a * LANES, (a + 1) * LANES)
                re = [wave[c, at : at + rows_at, lanes] for c in range(4)]
                im = [wave[c, quarter + at : quarter + at + rows_at, lanes] for c in range(4)]
                er, ei, fr, fi = re[0] + re[2], im[0] + im[2], re[0] - re[2], im[0] - im[2]
                gr, gi, hr, hi = re[1] + re[3], im[1] + im[3], re[1] - re[3], im[1] - im[3]
                outs = ((er + gr, ei + gi), (fr - hi, fi + hr), (er - gr, ei - gi), (fr + hi, fi - hr))
                for m, (w_re, w_im) in enumerate(outs):
                    mine = slice(m * quarter + at, m * quarter + at + rows_at)
                    p_re, p_im = probe[0, a, mine, :], probe[1, a, mine, :]
                    now[2 * m] = pltpu.roll(p_re * w_re + p_im * w_im, b, axis=1)
                    now[2 * m + 1] = pltpu.roll(p_re * w_im - p_im * w_re, b, axis=1)
            for k in range(8):
                rows = pl.ds(oy + (k // 2) * quarter + at, rows_at)
                sums[k % 2, q + a, rows, :] += jnp.where(lane >= b, now[k], before[k])
            before = now

    blocks = quarter // rows_at
    wave[...] = jnp.zeros_like(wave)
    for c in range(4):
        take_patch(0, c)

    def one_slot(s, carry):
        later, earlier = jnp.minimum(s + 1, amp_held.shape[0] - 1), jnp.maximum(s - 1, 0)
        amp_fetch(s).wait()
        for c in range(4):
            wide[c] = dot(rows_in[c], exits[c])
        step = quarter // 4
        for cc in range(4):
            for a in range(chunks):
                lanes = slice(a * LANES, (a + 1) * LANES)
                re = [wide[c, cc * step : (cc + 1) * step, lanes] for c in range(4)]
                im = [wide[c, quarter + cc * step : quarter + (cc + 1) * step, lanes] for c in range(4)]
                er, ei, fr, fi = re[0] + re[2], im[0] + im[2], re[0] - re[2], im[0] - im[2]
                gr, gi, hr, hi = re[1] + re[3], im[1] + im[3], re[1] - re[3], im[1] - im[3]
                outs = (
                    (er + gr, ei + gi),
                    (fr + hi, fi - hr),
                    (er - gr, ei - gi),
                    (fr - hi, fi + hr),
                )
                for m, (o_re, o_im) in enumerate(outs):
                    half[cc, m * step : (m + 1) * step, lanes] = o_re.astype(bf16)
                    half[cc, quarter + m * step : quarter + (m + 1) * step, lanes] = o_im.astype(bf16)

        for cc in range(4):
            wide[cc] = dot(half[cc], cols_in[...])
            take_patch(later, cc)
        mid = chunks // 2
        for cc in range(4):
            for part in range(mid):
                lo = slice(part * LANES, (part + 1) * LANES)
                hi = slice((mid + part) * LANES, (mid + part + 1) * LANES)
                p1, p3 = wide[cc, :quarter, lo], wide[cc, :quarter, hi]
                p4, p2 = wide[cc, quarter:, lo], wide[cc, quarter:, hi]
                if part == 0:
                    p2, p3 = jnp.where(lane == 0, -p3, p2), jnp.where(lane == 0, p2, p3)
                for sign in range(2):
                    s_re = p1 - p2 if sign == 0 else p1 + p2
                    s_im = p4 + p3 if sign == 0 else p4 - p3
                    at = (sign * mid + part) * LANES
                    measured = amp_held[s, cc * quarter : (cc + 1) * quarter, at : at + LANES].astype(f32)
                    inverse = jnp.minimum(lax.rsqrt(s_re * s_re + s_im * s_im), 1.0 / modulus_floor)
                    factor = measured * inverse - 1.0
                    rows = slice(cc * quarter, (cc + 1) * quarter)
                    for k, value in ((sign, s_re), (2 + sign, s_im)):
                        delta[part, rows, k * LANES : (k + 1) * LANES] = (value * factor).astype(bf16)

        for part in range(2):
            for r in range(2):
                wide[2 * part + r] = dot(delta[part, r * side // 2 : (r + 1) * side // 2, :], cols_out[part])
                for block in range(blocks // 4):
                    place_term(earlier, (2 * part + r) * (blocks // 4) + block)
        for cc in range(4):
            for k in range(2):
                for a in range(mid):
                    lanes = slice((k * mid + a) * LANES, (k * mid + a + 1) * LANES)
                    rows = slice((cc % 2) * quarter, (cc % 2 + 1) * quarter)
                    even, odd = wide[cc // 2, rows, lanes], wide[2 + cc // 2, rows, lanes]
                    put = slice(k * quarter, (k + 1) * quarter)
                    back[cc, put, a * LANES : (a + 1) * LANES] = (even + odd).astype(bf16)
                    back[cc, put, (mid + a) * LANES : (mid + a + 1) * LANES] = (even - odd).astype(bf16)

        for c in range(4):
            wave[c] = dot(rows_out[c], back[c])
        return carry

    lax.fori_loop(0, count_ref[0, 0], one_slot, 0)
    for r in range(blocks):
        place_term(count_ref[0, 0] - 1, r)

    scale = scale_ref[0, 0]
    for p in range(2):
        for a in range(chunks):
            lanes = slice(a * LANES, (a + 1) * LANES)
            right_out[p, :, lanes] = (scale * sums[p, chunks + a, :side, :]).astype(bf16)
            own_out[p, :, lanes] = held[p, a] + scale * sums[p, a, :side, :]
            at = side
            for rows, below_out, diag_out in zip(out_parts, below_outs, diag_outs):
                below_out[p, :, lanes] = scale * sums[p, a, at : at + rows, :]
                diag_out[p, :, lanes] = (scale * sums[p, chunks + a, at : at + rows, :]).astype(bf16)
                at += rows
        here = slice(p, p + 1)
        columns = (
            (left_out, 0, 0, True),
            (beside_out, chunks - 1, LANES - 1, True),
            (kept_out, chunks, 0, False),
            (second_out, 2 * chunks - 1, LANES - 1, False),
        )
        for target, a, at, with_own in columns:
            cells = scale * sums[p, a]
            turned = jnp.concatenate([cells[r * LANES : (r + 1) * LANES, :].T[at : at + 1, :] for r in range(2 * chunks)], axis=1)
            if with_own:
                own_turned = [held[p, a, r * LANES : (r + 1) * LANES, :].T[at : at + 1, :] for r in range(chunks)]
                turned += jnp.concatenate(own_turned + [jnp.zeros((1, side), f32)], axis=1)
            target[here, : 2 * side] = turned
        for k, row in enumerate((0, side - 1, side, 2 * side - 1)):
            for a in range(chunks):
                at = 2 * side + k * side + a * LANES
                mine = scale * sums[p, a, row : row + 1, :]
                if k < 2:
                    mine += held[p, a, row : row + 1, :]
                kept_out[here, at : at + LANES] = mine
                beside_out[here, at : at + LANES] = scale * sums[p, chunks + a, row : row + 1, :]


def order_kernel(amp_ref, pick_ref, out_ref, wide):
    side = pick_ref.shape[0]
    quarter = side // 4
    ordered = dot(amp_ref[0, 0], pick_ref[...])
    for a in range(side // LANES):
        lanes = slice(a * LANES, (a + 1) * LANES)
        wide[a] = ordered[:, lanes]
        for c in range(4):
            out_ref[0, c * quarter : (c + 1) * quarter, lanes] = wide[a, pl.ds(c, quarter, stride=4), :].astype(jnp.bfloat16)


def run_order(amplitude):
    slots, side = amplitude.shape[1], amplitude.shape[2]
    pick = transform_tables(side)[4]
    return pl.pallas_call(
        order_kernel,
        grid=(slots,),
        out_shape=jax.ShapeDtypeStruct((slots, side, side), jnp.bfloat16),
        in_specs=[
            pl.BlockSpec((1, 1, side, side), lambda s: (0, s, 0, 0)),
            pl.BlockSpec((side, side), lambda s: (0, 0)),
        ],
        out_specs=pl.BlockSpec((1, side, side), lambda s: (s, 0, 0)),
        scratch_shapes=[pltpu.VMEM((side // LANES, side, LANES), jnp.float32)],
        compiler_params=pltpu.CompilerParams(vmem_limit_bytes=8 * 2**20),
        cost_estimate=pl.CostEstimate(flops=2 * slots * side**3, bytes_accessed=4 * slots * side**2, transcendentals=0),
        name="order",
    )(amplitude, pick)


def run_slots(counts, offset_y, offset_x, scale, obj_re, obj_im, right, below, diag, probe_re, probe_im, amplitude, out_parts):
    side = probe_re.shape[0]
    chunks, quarter = side // LANES, side // 4
    f32, bf16 = jnp.float32, jnp.bfloat16
    tables = transform_tables(side)[:4]
    in_parts = [part.shape[1] for part in below]
    smem = pl.BlockSpec(memory_space=pltpu.SMEM)
    vmem = pl.BlockSpec(memory_space=pltpu.VMEM)
    here = pl.BlockSpec(memory_space=pl.ANY)
    slots = amplitude.shape[0]
    tile = lambda rows, kind: jax.ShapeDtypeStruct((2, rows, side), kind)
    outs = [tile(side, f32), tile(side, bf16)] + [jax.ShapeDtypeStruct((2, n * side), f32) for n in (2, 6, 6, 2)]
    outs += [tile(rows, f32) for rows in out_parts] + [tile(rows, bf16) for rows in out_parts]
    results = pl.pallas_call(
        functools.partial(slots_kernel, side, in_parts, out_parts),
        out_shape=outs,
        in_specs=[smem] * 4 + [here] * 2 + [vmem] * (1 + 2 * len(in_parts)) + [here] * 7,
        out_specs=[vmem] * len(outs),
        scratch_shapes=[
            pltpu.VMEM((2, 2 * chunks, 2 * side, LANES), f32),
            pltpu.VMEM((2, 2 * chunks, 2 * side, LANES), f32),
            pltpu.VMEM((2, chunks, side, LANES), f32),
            pltpu.VMEM((4, 2 * quarter, side), bf16),
            pltpu.VMEM((4, 2 * quarter, side), f32),
            pltpu.VMEM((4, 2 * quarter, side), bf16),
            pltpu.VMEM((2, side, side), bf16),
            pltpu.VMEM((4, 2 * quarter, side), bf16),
            pltpu.VMEM((2, chunks, side, LANES), f32),
            pltpu.VMEM((slots, side, side), bf16),
            pltpu.VMEM((4, 2 * quarter, side), f32),
            *[pltpu.VMEM(table.shape, bf16) for table in tables],
            pltpu.SemaphoreType.DMA((4 * chunks,)),
            pltpu.SemaphoreType.DMA((slots,)),
            pltpu.SemaphoreType.DMA((4,)),
        ],
        compiler_params=pltpu.CompilerParams(vmem_limit_bytes=46 * 2**20),
        name="slots",
    )(counts, offset_y, offset_x, scale, obj_re, obj_im, right, *below, *diag, probe_re, probe_im, amplitude, *tables)
    parts = len(out_parts)
    return results[0], results[1], results[2:6], results[6 : 6 + parts], results[6 + parts :]


def finish_kernel(parts, *refs):
    own_ref, right_ref = refs[:2]
    below_refs = refs[2 : 2 + len(parts)]
    up_ref, far_ref, down_ref, low_ref, left_ref, beside_ref, out_re, out_im, cells, spill, result, ring_ref = refs[
        2 + len(parts) :
    ]
    side = own_ref.shape[1]
    chunks = side // LANES
    f32 = jnp.float32
    pad, count = 16, 8
    rows = chunks + 2
    for p in range(2):
        for k, column in enumerate((left_ref, beside_ref)):
            for a in range(chunks):
                lanes = slice(a * LANES, (a + 1) * LANES)
                at = rows + k * chunks + a
                ring_ref[2 * k + p : 2 * k + p + 1, lanes] = column[p : p + 1, lanes] + up_ref[p, at : at + 1, :]
    ring = ring_ref[...].T
    for p in range(2):
        for a in range(chunks):
            lanes = slice(a * LANES, (a + 1) * LANES)
            at = 0
            for rows, below_ref in zip(parts, below_refs):
                mine = slice(at, at + rows)
                cells[p, a + 1, pad + at : pad + at + rows, :] = (
                    own_ref[p, mine, lanes] + right_ref[p, mine, lanes].astype(f32) + below_ref[p, :, lanes].astype(f32)
                )
                at += rows
        for k in range(2):
            beside = jnp.broadcast_to(ring[:, 2 * k + p : 2 * k + p + 1], (side, LANES))
            cells[p, k * (chunks + 1), pad : pad + side, :] = beside
        for a in range(chunks + 2):
            one = slice(a, a + 1)
            cells[p, a, pad - 1 : pad, :] = up_ref[p, one, :] + far_ref[p, one, :]
            cells[p, a, pad + side : pad + side + 1, :] = down_ref[p, one, :] + low_ref[p, one, :]

    bound = 2.0 * shrink_level
    lane = lax.broadcasted_iota(jnp.int32, (count, LANES), 1)
    even, first, last = lane % 2 == 0, lane == 0, lane == LANES - 1
    cut = lambda t: jnp.clip(t, -bound, bound)
    later = lambda t: pltpu.roll(t, 1, axis=1)
    sooner = lambda t: pltpu.roll(t, LANES - 1, axis=1)

    def clips(total, gap, total_x, gap_x):
        side_by_side = cut(total - total_x)
        other = cut(gap + gap_x) + cut(gap - gap_x)
        return side_by_side + other, side_by_side - other

    def moved(p, at):
        upper = pl.ds(pad + 1 + 2 * at, count, stride=2)
        lower = pl.ds(pad + 2 + 2 * at, count, stride=2)
        high = [cells[p, a, upper, :] for a in range(chunks + 2)]
        low = [cells[p, a, lower, :] for a in range(chunks + 2)]
        fields = [[h + w for h, w in zip(high, low)], [h - w for h, w in zip(high, low)]]
        turned = []
        for field in fields:
            right_of = [later(field[a]) for a in range(chunks + 1)]
            left_of = [sooner(field[a]) for a in range(1, chunks + 2)]
            turned.append(
                [
                    jnp.where(
                        even,
                        jnp.where(first, right_of[a - 1], right_of[a]),
                        jnp.where(last, left_of[a], left_of[a - 1]),
                    )
                    for a in range(1, chunks + 1)
                ]
            )
        return [clips(fields[0][a + 1], fields[1][a + 1], turned[0][a], turned[1][a]) for a in range(chunks)]

    for p in range(2):
        for a, (_, below_one) in enumerate(moved(p, -count)):
            spill[p, a, 1 : 1 + count, :] = below_one

    def block(i, carry):
        at = pl.multiple_of(i * count, count)
        for p in range(2):
            shifted_clips = moved(p, at)
            for a in range(chunks):
                upper = pl.ds(pad + 2 * at, count, stride=2)
                lower = pl.ds(pad + 1 + 2 * at, count, stride=2)
                high, low = cells[p, a + 1, upper, :], cells[p, a + 1, lower, :]
                total, gap = high + low, high - low
                total_x = jnp.where(even, sooner(total), later(total))
                gap_x = jnp.where(even, sooner(gap), later(gap))
                top_clip, low_clip = clips(total, gap, total_x, gap_x)
                spill[p, a, pl.ds(at + count + 1, count), :] = shifted_clips[a][1]
                top_clip += spill[p, a, pl.ds(at + count, count), :]
                low_clip += shifted_clips[a][0]
                result[p, a, pl.ds(2 * at, count, stride=2), :] = high - 0.125 * top_clip
                result[p, a, pl.ds(2 * at + 1, count, stride=2), :] = low - 0.125 * low_clip
            for a in range(chunks):
                mine = pl.ds(2 * at, 2 * count)
                (out_re, out_im)[p][mine, a * LANES : (a + 1) * LANES] = result[p, a, mine, :]
        return carry

    lax.fori_loop(0, side // (2 * count), block, 0, unroll=UNROLL)


def run_finish(own, right, below, *edges):
    side = own.shape[1]
    chunks = side // LANES
    f32 = jnp.float32
    vmem = pl.BlockSpec(memory_space=pltpu.VMEM)
    tile = jax.ShapeDtypeStruct((side, side), f32)
    parts = [part.shape[1] for part in below]
    return pl.pallas_call(
        functools.partial(finish_kernel, parts),
        out_shape=(tile, tile),
        in_specs=[vmem] * (2 + len(parts) + len(edges)),
        out_specs=[vmem] * 2,
        scratch_shapes=[
            pltpu.VMEM((2, chunks + 2, side + 32, LANES), f32),
            pltpu.VMEM((2, chunks, side // 2 + 16, LANES), f32),
            pltpu.VMEM((2, chunks, side, LANES), f32),
            pltpu.VMEM((8, side), f32),
        ],
        compiler_params=pltpu.CompilerParams(vmem_limit_bytes=20 * 2**20),
        name="finish",
    )(own, right, *below, *edges)


def ring_kernel(right_ref, left_ref, second_ref, kept_ref, far_out, down_out, up_out, low_out, beside_left, beside_right):
    side = right_ref.shape[1] // 2
    chunks = side // LANES
    both = slice(0, 2 * side)
    beside_left[...] = left_ref[:, both] + second_ref[...]
    beside_right[...] = right_ref[...] + kept_ref[:, both]
    for k, (target, at) in enumerate(((up_out, 0), (down_out, side - 1), (low_out, side), (far_out, 2 * side - 1))):
        for p in range(2):
            here = slice(p, p + 1)
            for row, column in ((0, beside_left), (chunks + 1, beside_right)):
                target[p, row : row + 1, :] = jnp.broadcast_to(column[here, at : at + 1], (1, LANES))
            for a in range(chunks):
                lanes = slice(2 * side + k * side + a * LANES, 2 * side + k * side + (a + 1) * LANES)
                target[p, a + 1 : a + 2, :] = kept_ref[here, lanes] + left_ref[here, lanes]
    for p in range(2):
        for k, column in enumerate((beside_left, beside_right)):
            for a in range(chunks):
                row = chunks + 2 + k * chunks + a
                lanes = slice(side + a * LANES, side + (a + 1) * LANES)
                down_out[p, row : row + 1, :] = column[p : p + 1, lanes]


def run_ring(right, left, second, kept):
    wide = right.shape[1]
    chunks = wide // 2 // LANES
    vmem = pl.BlockSpec(memory_space=pltpu.VMEM)
    rows = [chunks + 2, 3 * chunks + 2, chunks + 2, chunks + 2]
    shapes = [(2, n, LANES) for n in rows] + [(2, wide)] * 2
    return pl.pallas_call(
        ring_kernel,
        out_shape=[jax.ShapeDtypeStruct(shape, jnp.float32) for shape in shapes],
        in_specs=[vmem] * 4,
        out_specs=[vmem] * 6,
        compiler_params=pltpu.CompilerParams(vmem_limit_bytes=2 * 2**20),
        name="ring",
    )(right, left, second, kept)


def shifted(value, axis, steps):
    count = lax.axis_size(axis)
    return lax.ppermute(value, axis, [(i, (i + steps) % count) for i in range(count)])


def parts_of(side, weights):
    unit = side // 32
    sizes = [unit * weight for weight in weights]
    assert sum(sizes) == side and unit % 16 == 0
    return sizes


def split_rows(value, sizes):
    ends = np.cumsum(sizes)
    return [value[:, end - size : end] for end, size in zip(ends, sizes)]


def update(obj_re, obj_im, probe_re, probe_im, amplitude, offset_y, offset_x, counts):
    f32, bf16 = jnp.float32, jnp.bfloat16
    side = probe_re.shape[0]
    in_parts, out_parts = parts_of(side, IN_SHARES), parts_of(side, OUT_SHARES)

    head = in_parts[0]
    piece = jnp.stack([obj_re[:head], obj_im[:head]]).astype(bf16)
    piece, later_re, later_im = lax.optimization_barrier((piece, obj_re, obj_im))
    below = [shifted(piece, "row", -1)]
    own = jnp.stack([later_re, later_im]).astype(bf16)
    right = shifted(own, "col", -1)
    for rest in split_rows(own, in_parts)[1:]:
        below.append(shifted(rest, "row", -1))
    diag = [shifted(value, "col", -1) for value in below]
    amplitude = run_order(amplitude)
    probe_power = jnp.mean(probe_re * probe_re + probe_im * probe_im) + epsilon
    scale = (step_size / probe_power).reshape(1, 1)
    own_sum, right_sum, edges, below_sum, diag_sum = run_slots(
        counts, offset_y, offset_x, scale, obj_re, obj_im, right, below, diag, probe_re, probe_im, amplitude, out_parts
    )

    to_left, to_right, kept, to_second = edges
    diag_in = [shifted(value, "col", 1) for value in diag_sum]
    ring_parts = (shifted(to_left, "col", -1), shifted(to_right, "col", 1), shifted(to_second, "col", 2))
    right_in = shifted(right_sum, "col", 1)
    below_in = []
    for mine, theirs in zip(below_sum, diag_in):
        sent = (mine + theirs.astype(f32)).astype(bf16)
        below_in.append(shifted(sent, "row", 1))
    low_last, sent_down, first, low_first, beside_left, beside_right = run_ring(*ring_parts, kept)
    from_far = shifted(low_last, "row", 2)
    from_up = shifted(sent_down, "row", 1)
    from_down = shifted(first, "row", -1)
    return run_finish(own_sum, right_in, below_in, from_up, from_far, from_down, low_first, beside_left, beside_right)


IN_SHARES = (16, 8, 5, 3)
OUT_SHARES = (5, 9, 18)


def solution(mesh):
    split = P("row", "col")
    return jax.shard_map(
        update,
        mesh=mesh,
        in_specs=(split, split, P(), P(), P("row", "col", None, None), split, split, split),
        out_specs=(split, split),
        check_vma=False,
    )
```
